256 devices in a mesh: gx: 8 (over z_lo, core), gy: 8 (over y, z_hi), gz: 4 (over x).
Axes of the slice: x: 4, y: 4, z: 8 (z_hi: 2, z_lo: 4; z = z_hi * 4 + z_lo), core: 2. Of those that a mesh axis runs over, the one named last changes fastest.
Arguments:
- positions: float32 [3, 32, 32, 8, 128], P(None, 'gx', 'gy', 'gz'), may hold values from 0 to 1
- line_vectors: float32 [3, 32, 32, 8, 128], P(None, 'gx', 'gy', 'gz'), may hold values from -3 to 3
- burgers: float32 [3, 32, 32, 8, 128], P(None, 'gx', 'gy', 'gz'), may hold values from -6 to 6
- mobility: float32 [32, 32, 8, 128], P('gx', 'gy', 'gz'), may hold values from 0.25 to 4
- occupancy: int32 [32, 32, 8], P('gx', 'gy', 'gz'), may hold values from 1 to 128
Outputs:
- moved_positions: float32 [3, 32, 32, 8, 128], P(None, 'gx', 'gy', 'gz')
- end_forces: float32 [3, 32, 32, 8, 128], P(None, 'gx', 'gy', 'gz')
The draws below stay inside these ranges and needn't reach their ends.
All inputs are finite; a program needn't handle non-finite values.
Results may differ from the reference program's by a relative error of at most 0.0001.
Values sent between devices are 32-bit elements; how exact they have to be, the bound alone decides.
No kernel may reach another device: no remote copies, remote signals or barrier semaphores. Data moves between devices by JAX's collectives and lax.ppermute only.
A program may use at most 64 MiB of HBM per device.

```python
import math
import jax
import jax.numpy as jnp
from jax import lax

SLOTS = 128
NCX = 32
NCY = 32
NCZ = 8


def place_ends(values, own_key, least, largest):
    dims = values.shape
    spot = [jax.random.randint(jax.random.fold_in(own_key, axis), (), 0, dims[axis]) for axis in range(len(dims))]
    values = values.at[tuple(spot)].set(least)
    longest = dims.index(max(dims))
    spot[longest] = (spot[longest] + 1) % dims[longest]
    return values.at[tuple(spot)].set(largest)


def steps_of(stream_key, shape, cuts, smallest, largest):
    def one(axis_at, blocks):
        steps = jax.random.uniform(jax.random.fold_in(jax.random.fold_in(stream_key, 6), axis_at), (blocks,), jnp.float32, smallest / len(cuts), largest / len(cuts))
        return jnp.repeat(jnp.exp(steps), shape[axis_at] // blocks).reshape((-1,) + (1,) * (len(shape) - axis_at - 1))

    level = one(*cuts[0])
    for cut in cuts[1:]:
        level = level * one(*cut)
    return level


def scatter_about(own_key, shape, scale, most, cuts=(), dtype=jnp.bfloat16):
    factor_of = steps_of(own_key, shape, cuts, -0.22, 0.18) if cuts else 1.0
    drawn = jax.random.normal(own_key, shape, jnp.float32) * scale * factor_of
    return jnp.minimum(jnp.maximum(drawn, -most), most).astype(dtype)


def setup_inputs(seed: int = 0) -> dict:
    arg_keys = jax.random.split(jax.random.key(seed), 6)
    return {
        "positions": jnp.clip(1.0 * jax.random.uniform(arg_keys[0], (3, NCX, NCY, NCZ, SLOTS), jnp.float32) ** steps_of(arg_keys[0], (3, NCX, NCY, NCZ, SLOTS), ((1, 8), (2, 8), (3, 4)), -0.2, 0.2), 0.0, 1.0),
        "line_vectors": scatter_about(arg_keys[1], (3, NCX, NCY, NCZ, SLOTS), 0.5, 3.0, ((1, 8), (2, 8), (3, 4)), jnp.float32),
        "burgers": scatter_about(arg_keys[2], (3, NCX, NCY, NCZ, SLOTS), 1.0, 6.0, ((1, 8), (2, 8), (3, 4)), jnp.float32),
        "mobility": jnp.clip(jnp.exp(math.log(4.0) - 2.7725887 * jax.random.uniform(arg_keys[3], (NCX, NCY, NCZ, SLOTS), jnp.float32) ** steps_of(arg_keys[3], (NCX, NCY, NCZ, SLOTS), ((0, 8), (1, 8), (2, 4)), -0.2, 0.2)), 0.25, 4.0),
        "occupancy": place_ends(jax.random.randint(arg_keys[4], (NCX, NCY, NCZ), 1, SLOTS + 1), jax.random.fold_in(arg_keys[4], 1), 1, SLOTS).astype(jnp.int32),
    }


CORE_SQUARED = 0.25
MU_SCALE = 0.05
CROSS_WEIGHT = 0.5
STEP_LIMIT = 0.1
NEIGHBOUR_SHIFTS = [(first, second, third) for first in (-1, 0, 1) for second in (-1, 0, 1) for third in (-1, 0, 1)]

def inner_pairs(left, right):
    return sum((left[k][..., :, None] * right[k][..., None, :] for k in range(3)))

def tile_force(target, source, offset):
    separate = [target[k][..., :, None] - source[k][..., None, :] - float(offset[k]) for k in range(3)]
    radius_sq = separate[0] * separate[0] + separate[1] * separate[1] + separate[2] * separate[2] + CORE_SQUARED
    inverse = lax.rsqrt(radius_sq)
    couple = inner_pairs(target[6:9], source[6:9]) * inner_pairs(target[3:6], source[3:6])
    couple = couple - CROSS_WEIGHT * inner_pairs(target[6:9], source[3:6]) * inner_pairs(target[3:6], source[6:9])
    weight = couple * source[9][..., None, :] * inverse * inverse * inverse
    return jnp.stack([lax.optimization_barrier(jnp.sum(weight * separate[k], axis=-1)) for k in range(3)]) * (MU_SCALE * target[9])

def all_forces(fields):
    total = jnp.zeros((3,) + fields.shape[1:], jnp.float32)
    for offset in NEIGHBOUR_SHIFTS:
        source = jnp.roll(fields, (-offset[0], -offset[1], -offset[2]), (1, 2, 3))
        both = jnp.moveaxis(jnp.stack([fields, source]), 2, 0)
        slabs = lax.map(lambda pair: tile_force(pair[0], pair[1], offset), both)
        total = total + jnp.moveaxis(slabs, 0, 1)
    return total

def reference(positions, line_vectors, burgers, mobility, occupancy):
    slots = lax.broadcasted_iota(jnp.int32, mobility.shape, 3)
    live = (slots < occupancy[..., None]).astype(jnp.float32)
    fixed_part = jnp.concatenate([line_vectors, burgers, live[None]], 0)
    start_forces = all_forces(jnp.concatenate([positions, fixed_part], 0))
    speed0 = mobility[None] * start_forces
    peak = jnp.max(lax.optimization_barrier(jnp.sum(speed0 * speed0, axis=0)))
    step = STEP_LIMIT * lax.rsqrt(peak + 1e-12)
    predicted = positions + step * speed0
    end_forces = all_forces(jnp.concatenate([predicted, fixed_part], 0))
    moved_positions = positions + 0.5 * step * (speed0 + mobility[None] * end_forces)
    return (moved_positions, end_forces)
```

```python
import functools

import jax
import jax.numpy as jnp
from jax import lax
from jax.experimental import pallas as pl
from jax.experimental.pallas import tpu as pltpu
from jax.sharding import Mesh
from jax.sharding import PartitionSpec as P

GX = ("gx_0", "gx_1")
GY = ("gy_0", "gy_1")
EVERY = ("gx_0", "gx_1", "gy_0", "gy_1", "gz")

CORE_SQUARED = 0.25
MU_SCALE = 0.05
CROSS_WEIGHT = 0.5
STEP_LIMIT = 0.1

NX, NY, NZ, SLOTS = 4, 4, 2, 128
PX, PY, PZ = NX + 2, NY + 2, NZ + 2
CELLS = NX * NY * NZ
PADDED = PX * PY * PZ
KF = 32
VF = 40
VROWS = 128
F32 = jnp.float32
BF16 = jnp.bfloat16


def ring(axis):
    count = lax.axis_size(axis)
    forward = [(i, (i + 1) % count) for i in range(count)]
    return forward, [(t, s) for s, t in forward]


def extended(block, sides):
    for axis, dim in sides:
        forward, backward = ring(axis)
        size = block.shape[dim]
        low = lax.ppermute(lax.slice_in_dim(block, size - 1, size, axis=dim), axis, forward)
        high = lax.ppermute(lax.slice_in_dim(block, 0, 1, axis=dim), axis, backward)
        block = jnp.concatenate([low, block, high], axis=dim)
    return block


def parts3(v):
    high = v.astype(BF16).astype(F32)
    rest = v - high
    mid = rest.astype(BF16).astype(F32)
    return high, mid, rest - mid


def distance_features(coords, source):
    one = jnp.ones_like(coords[0])
    square = coords[0] * coords[0] + coords[1] * coords[1] + coords[2] * coords[2]
    rows = []
    for x in coords:
        h, m, l = parts3(x)
        if source:
            h, m, l = -2.0 * h, -2.0 * m, -2.0 * l
            rows += [h, h, m, m, h, l]
        else:
            rows += [h, m, h, m, l, h]
    if source:
        rows += [*parts3(square), one, one, one]
    else:
        rows += [one, one, one, *parts3(square + CORE_SQUARED)]
    return rows + [jnp.zeros_like(one)] * (KF - len(rows))


def prepare_sources(pad_ref, shift, pf, vf):
    sub = lax.broadcasted_iota(jnp.int32, (8, SLOTS), 0)
    y_in = (sub >> 2).astype(F32)
    z_in = (sub & 3).astype(F32)

    def group(g, carry):
        rows = pl.ds(pl.multiple_of(g * 8, 8), 8)
        x0 = (g // 3).astype(F32) - float(PX // 2)
        y0 = ((g % 3) * 2).astype(F32) - float(PY // 2)
        pos = [pad_ref[a, rows, :] for a in range(3)]
        if shift is not None:
            padv_ref, step = shift
            pos = [pos[a] + step * padv_ref[a, rows, :] for a in range(3)]
        coords = [pos[0] + x0, pos[1] + (y_in + y0), pos[2] + (z_in - float(PZ // 2))]
        for f, row in enumerate(distance_features(coords, True)):
            pf[pl.ds(g * (8 * KF) + f, 8, stride=KF), :] = row
        line = [pad_ref[3 + a, rows, :] for a in range(3)]
        live = pad_ref[9, rows, :]
        burg = [pad_ref[6 + a, rows, :] * live for a in range(3)]
        outer = [[burg[m] * line[n] for n in range(3)] for m in range(3)]
        for m in range(3):
            for n in range(3):
                b = outer[m][n] - CROSS_WEIGHT * outer[n][m]
                f = 3 * m + n
                vf[pl.ds(g * (8 * VF) + f, 8, stride=VF), :] = b
                for a in range(3):
                    at = g * (8 * VF) + 9 * (a + 1) + f
                    vf[pl.ds(at, 8, stride=VF), :] = b * coords[a]
        return carry

    lax.fori_loop(0, PADDED // 8, group, 0)


def lay_out_sources(pf, vf, pt, vt):
    def column(c, carry):
        at = pl.multiple_of(c * 128, 128)
        pt[pl.ds(at, 128), :] = pf[pl.ds(at, 128), :].T.astype(BF16)
        x, y = c // PY, c % PY
        lanes = pl.ds(pl.multiple_of(y * SLOTS, SLOTS), SLOTS)
        for z in range(PZ):
            v = vf[pl.ds(pl.multiple_of(c * (PZ * VF) + z * VF, 8), VF), :]
            rows = [*parts3(v), jnp.zeros((VROWS - 3 * VF, SLOTS), F32)]
            vt[x, z, :, lanes] = jnp.concatenate(rows, 0).astype(BF16)
        return carry

    lax.fori_loop(0, PX * PY, column, 0)


def prepare_targets(loc_ref, shift, qf):
    sub = lax.broadcasted_iota(jnp.int32, (8, SLOTS), 0)
    y_in = (sub >> 1).astype(F32)
    z_in = (sub & 1).astype(F32)
    every = []
    for g in range(CELLS // 8):
        rows = pl.ds(g * 8, 8)
        pos = [loc_ref[a, rows, :] for a in range(3)]
        if shift is not None:
            speed_ref, step = shift
            pos = [pos[a] + step * speed_ref[a, rows, :] for a in range(3)]
        coords = [
            pos[0] + float(g + 1 - PX // 2),
            pos[1] + (y_in + float(1 - PY // 2)),
            pos[2] + (z_in + float(1 - PZ // 2)),
        ]
        for f, row in enumerate(distance_features(coords, False)):
            qf[pl.ds(g * (8 * KF) + f, 8, stride=KF), :] = row
        every.append(coords)
    return every


def pair_sums(pt, vt, qf, tf):
    span = 3 * SLOTS
    diag = lax.broadcasted_iota(jnp.int32, (SLOTS, SLOTS), 0) == lax.broadcasted_iota(
        jnp.int32, (SLOTS, SLOTS), 1
    )
    zero = jnp.zeros((KF, 2 * SLOTS), BF16)
    half = jnp.zeros((KF, SLOTS), BF16)

    def split(s):
        inverse = lax.rsqrt(s)
        g = inverse * inverse * inverse
        return g

    def parts2(g):
        high = g.astype(BF16)
        return high, (g - high.astype(F32)).astype(BF16)

    def target(c, carry):
        x, y = c // NY, c % NY
        q0 = qf[pl.ds(pl.multiple_of(c * (2 * KF), 8), KF), :].astype(BF16)
        q1 = qf[pl.ds(pl.multiple_of(c * (2 * KF) + KF, 8), KF), :].astype(BF16)
        both = jnp.concatenate([q0, q1], 1)
        ends = [jnp.concatenate([q0, half], 1), jnp.concatenate([half, q1], 1)]
        weights = [
            jnp.concatenate([zero, both, zero, zero], 0),
            jnp.concatenate([zero, zero, both, zero], 0),
            jnp.concatenate([ends[0], zero, zero, ends[1]], 0),
        ]
        lanes = pl.ds(pl.multiple_of(y * SLOTS, SLOTS), span)
        total = jnp.zeros((VROWS, 2 * SLOTS), F32)
        for dx in range(3):
            rows = pl.ds(pl.multiple_of(((x + dx) * PY + y) * SLOTS, SLOTS), span)
            source = pt[rows, :]
            for tile in range(3):
                s = jnp.dot(source, weights[tile], preferred_element_type=F32)
                g = split(s)
                if dx == 1 and tile < 2:
                    mid = g[SLOTS : 2 * SLOTS]
                    own = jnp.where(diag, 0.0, mid[:, tile * SLOTS : (tile + 1) * SLOTS])
                    other = mid[:, (1 - tile) * SLOTS : (2 - tile) * SLOTS]
                    mid = jnp.concatenate([own, other] if tile == 0 else [other, own], 1)
                    g = jnp.concatenate([g[:SLOTS], mid, g[2 * SLOTS :]], 0)
                high, low = parts2(g)
                if tile < 2:
                    v = vt[x + dx, tile + 1, :, lanes]
                    total = total + jnp.dot(v, high, preferred_element_type=F32)
                    total = total + jnp.dot(v, low, preferred_element_type=F32)
                else:
                    ends_sum = []
                    for t in range(2):
                        v = vt[x + dx, 3 * t, :, lanes]
                        col = slice(t * SLOTS, (t + 1) * SLOTS)
                        ends_sum.append(
                            jnp.dot(v, high[:, col], preferred_element_type=F32)
                            + jnp.dot(v, low[:, col], preferred_element_type=F32)
                        )
                    total = total + jnp.concatenate(ends_sum, 1)
        sums = total[0:VF] + total[VF : 2 * VF] + total[2 * VF : 3 * VF]
        for t in range(2):
            at = pl.multiple_of(c * (2 * VF) + t * VF, 8)
            tf[pl.ds(at, VF), :] = sums[:, t * SLOTS : (t + 1) * SLOTS]
        return carry

    lax.fori_loop(0, NX * NY, target, 0)


def forces_of(g, coords, loc_ref, tf):
    rows = pl.ds(g * 8, 8)
    line = [loc_ref[3 + a, rows, :] for a in range(3)]
    burg = [loc_ref[6 + a, rows, :] for a in range(3)]
    live = loc_ref[9, rows, :]
    sums = [jnp.zeros((8, SLOTS), F32) for _ in range(4)]
    for m in range(3):
        for n in range(3):
            a = burg[m] * line[n]
            for k in range(4):
                at = g * (8 * VF) + 9 * k + 3 * m + n
                sums[k] = sums[k] + a * tf[pl.ds(at, 8, stride=VF), :]
    scale = MU_SCALE * live
    return [scale * (coords[k] * sums[0] - sums[k + 1]) for k in range(3)]


def start_kernel(pad_ref, loc_ref, mob_ref, speed_ref, peak_ref, pf, vf, pt, vt, qf, tf):
    prepare_sources(pad_ref, None, pf, vf)
    lay_out_sources(pf, vf, pt, vt)
    every = prepare_targets(loc_ref, None, qf)
    pair_sums(pt, vt, qf, tf)
    peak = jnp.zeros((8, SLOTS), F32)
    for g in range(CELLS // 8):
        rows = pl.ds(g * 8, 8)
        force = forces_of(g, every[g], loc_ref, tf)
        mobility = mob_ref[rows, :]
        speed = [mobility * f for f in force]
        for a in range(3):
            speed_ref[a, rows, :] = speed[a]
        peak = jnp.maximum(
            peak, speed[0] * speed[0] + speed[1] * speed[1] + speed[2] * speed[2]
        )
    top = jnp.max(jnp.max(peak, axis=0, keepdims=True), axis=1, keepdims=True)
    peak_ref[...] = jnp.broadcast_to(top, peak_ref.shape)


def end_kernel(
    pad_ref, loc_ref, mob_ref, padv_ref, speed_ref, peak_ref, moved_ref, force_ref,
    pf, vf, pt, vt, qf, tf,
):
    peak = jnp.max(jnp.max(peak_ref[...], axis=0, keepdims=True), axis=1, keepdims=True)
    step = STEP_LIMIT * lax.rsqrt(jnp.broadcast_to(peak, (8, SLOTS)) + 1e-12)
    prepare_sources(pad_ref, (padv_ref, step), pf, vf)
    lay_out_sources(pf, vf, pt, vt)
    every = prepare_targets(loc_ref, (speed_ref, step), qf)
    pair_sums(pt, vt, qf, tf)
    for g in range(CELLS // 8):
        rows = pl.ds(g * 8, 8)
        force = forces_of(g, every[g], loc_ref, tf)
        mobility = mob_ref[rows, :]
        for a in range(3):
            force_ref[a, rows, :] = force[a]
            moved_ref[a, rows, :] = loc_ref[a, rows, :] + 0.5 * step * (
                speed_ref[a, rows, :] + mobility * force[a]
            )


def call(kernel, out_shapes, operands, name):
    whole = pl.BlockSpec(memory_space=pltpu.VMEM)
    return pl.pallas_call(
        kernel,
        out_shape=out_shapes,
        in_specs=[whole] * len(operands),
        out_specs=[whole] * len(out_shapes),
        scratch_shapes=[
            pltpu.VMEM((PADDED * KF, SLOTS), F32),
            pltpu.VMEM((PADDED * VF, SLOTS), F32),
            pltpu.VMEM((PX * PY * SLOTS, 128), BF16),
            pltpu.VMEM((PX, PZ, VROWS, PY * SLOTS), BF16),
            pltpu.VMEM((CELLS * KF, SLOTS), F32),
            pltpu.VMEM((CELLS * VF, SLOTS), F32),
        ],
        compiler_params=pltpu.CompilerParams(vmem_limit_bytes=48 << 20),
        name=name,
    )(*operands)


def on_device(positions, line_vectors, burgers, mobility, occupancy):
    slots = lax.broadcasted_iota(jnp.int32, mobility.shape, 3)
    live = (slots < occupancy[..., None]).astype(F32)
    fields = jnp.concatenate([positions, line_vectors, burgers, live[None]], 0)
    sides = ((GX, 1), (GY, 2), ("gz", 3))
    pad = extended(fields, sides).reshape(10, PADDED, SLOTS)
    loc = fields.reshape(10, CELLS, SLOTS)
    mob = mobility.reshape(CELLS, SLOTS)
    devices = lax.axis_size(EVERY)
    vec = jax.ShapeDtypeStruct((3, CELLS, SLOTS), F32)
    speed, peaks = call(
        start_kernel,
        [vec, jax.ShapeDtypeStruct((devices, SLOTS), F32)],
        [pad, loc, mob],
        "start_forces",
    )
    peaks = lax.all_to_all(peaks.reshape(devices, 1, SLOTS), EVERY, 0, 0)
    peaks = peaks.reshape(devices, SLOTS)
    padv = extended(speed.reshape(3, NX, NY, NZ, SLOTS), sides).reshape(3, PADDED, SLOTS)
    moved, force = call(
        end_kernel, [vec, vec], [pad, loc, mob, padv, speed, peaks], "end_forces"
    )
    shape = (3, NX, NY, NZ, SLOTS)
    return moved.reshape(shape), force.reshape(shape)


def solution(mesh):
    finer = Mesh(
        mesh.devices.reshape(4, 2, 4, 2, mesh.shape["gz"]), ("gx_0", "gx_1", "gy_0", "gy_1", "gz")
    )
    in_specs = (
        P(None, GX, GY, "gz", None),
        P(None, GX, GY, "gz", None),
        P(None, GX, GY, "gz", None),
        P(GX, GY, "gz", None),
        P(GX, GY, "gz"),
    )
    out_specs = (P(None, GX, GY, "gz", None), P(None, GX, GY, "gz", None))
    return jax.shard_map(
        on_device, mesh=finer, in_specs=in_specs, out_specs=out_specs, check_vma=False
    )
```

```python
import functools

import jax
import jax.numpy as jnp
from jax import lax
from jax.experimental import pallas as pl
from jax.experimental.pallas import tpu as pltpu
from jax.sharding import Mesh
from jax.sharding import PartitionSpec as P

GX = ("gx_0", "gx_1")
GY = ("gy_0", "gy_1")
EVERY = ("gx_0", "gx_1", "gy_0", "gy_1", "gz")

CORE_SQUARED = 0.25
MU_SCALE = 0.05
CROSS_WEIGHT = 0.5
STEP_LIMIT = 0.1

NX, NY, NZ, SLOTS = 4, 4, 2, 128
PX, PY, PZ = NX + 2, NY + 2, NZ + 2
CELLS = NX * NY * NZ
PADDED = PX * PY * PZ
UNROLL_L, UNROLL_P = 6, 1
KF = 32
VF = 40
FAR = 3e38
VROWS = 128
F32 = jnp.float32
BF16 = jnp.bfloat16


def ring(axis):
    count = lax.axis_size(axis)
    forward = [(i, (i + 1) % count) for i in range(count)]
    return forward, [(t, s) for s, t in forward]


def extended(block, sides):
    for axis, dim in sides:
        forward, backward = ring(axis)
        size = block.shape[dim]
        low = lax.ppermute(lax.slice_in_dim(block, size - 1, size, axis=dim), axis, forward)
        high = lax.ppermute(lax.slice_in_dim(block, 0, 1, axis=dim), axis, backward)
        block = jnp.concatenate([low, block, high], axis=dim)
    return block


def parts3(v):
    high = v.astype(BF16).astype(F32)
    rest = v - high
    mid = rest.astype(BF16).astype(F32)
    return high, mid, rest - mid


def distance_features(coords, source):
    one = jnp.ones_like(coords[0])
    square = coords[0] * coords[0] + coords[1] * coords[1] + coords[2] * coords[2]
    rows = []
    for x in coords:
        h, m, l = parts3(x)
        if source:
            h, m, l = -2.0 * h, -2.0 * m, -2.0 * l
            rows += [h, h, m, m, h, l]
        else:
            rows += [h, m, h, m, l, h]
    if source:
        rows += [*parts3(square), one, one, one]
    else:
        rows += [one, one, one, *parts3(square + CORE_SQUARED)]
    return rows + [jnp.zeros_like(one)] * (KF - len(rows))


def prepare_sources(pad_ref, shift, pf, vf):
    sub = lax.broadcasted_iota(jnp.int32, (8, SLOTS), 0)
    y_in = (sub >> 2).astype(F32)
    z_in = (sub & 3).astype(F32)

    def group(g, carry):
        rows = pl.ds(pl.multiple_of(g * 8, 8), 8)
        x0 = (g // 3).astype(F32) - float(PX // 2)
        y0 = ((g % 3) * 2).astype(F32) - float(PY // 2)
        pos = [pad_ref[a, rows, :] for a in range(3)]
        if shift is not None:
            padv_ref, step = shift
            pos = [pos[a] + step * padv_ref[a, rows, :] for a in range(3)]
        coords = [pos[0] + x0, pos[1] + (y_in + y0), pos[2] + (z_in - float(PZ // 2))]
        for f, row in enumerate(distance_features(coords, True)):
            pf[pl.ds(g * (8 * KF) + f, 8, stride=KF), :] = row
        line = [pad_ref[3 + a, rows, :] for a in range(3)]
        burg = [pad_ref[6 + a, rows, :] for a in range(3)]
        outer = [[burg[m] * line[n] for n in range(3)] for m in range(3)]
        for m in range(3):
            for n in range(3):
                b = outer[m][n] - CROSS_WEIGHT * outer[n][m]
                f = 3 * m + n
                vf[pl.ds(g * (8 * VF) + f, 8, stride=VF), :] = b
                for a in range(3):
                    at = g * (8 * VF) + 9 * (a + 1) + f
                    vf[pl.ds(at, 8, stride=VF), :] = b * coords[a]
        return carry

    lax.fori_loop(0, PADDED // 8, group, 0, unroll=UNROLL_P)


def lay_out_sources(pf, vf, pt, vt):
    def column(c, carry):
        at = pl.multiple_of(c * 128, 128)
        pt[pl.ds(at, 128), :] = pf[pl.ds(at, 128), :].T.astype(BF16)
        x, y = c // PY, c % PY
        lanes = pl.ds(pl.multiple_of(y * SLOTS, SLOTS), SLOTS)
        for z in range(PZ):
            v = vf[pl.ds(pl.multiple_of(c * (PZ * VF) + z * VF, 8), VF), :]
            rows = [*parts3(v), jnp.zeros((VROWS - 3 * VF, SLOTS), F32)]
            vt[x, z, :, lanes] = jnp.concatenate(rows, 0).astype(BF16)
        return carry

    lax.fori_loop(0, PX * PY, column, 0, unroll=UNROLL_L)


def prepare_targets(loc_ref, shift, qf):
    sub = lax.broadcasted_iota(jnp.int32, (8, SLOTS), 0)
    y_in = (sub >> 1).astype(F32)
    z_in = (sub & 1).astype(F32)
    every = []
    for g in range(CELLS // 8):
        rows = pl.ds(g * 8, 8)
        pos = [loc_ref[a, rows, :] for a in range(3)]
        if shift is not None:
            speed_ref, step = shift
            pos = [pos[a] + step * speed_ref[a, rows, :] for a in range(3)]
        coords = [
            pos[0] + float(g + 1 - PX // 2),
            pos[1] + (y_in + float(1 - PY // 2)),
            pos[2] + (z_in + float(1 - PZ // 2)),
        ]
        for f, row in enumerate(distance_features(coords, False)):
            qf[pl.ds(g * (8 * KF) + f, 8, stride=KF), :] = row
        every.append(coords)
    return every


def parts2(s):
    inverse = lax.rsqrt(s)
    g = inverse * inverse * inverse
    high = g.astype(BF16)
    return high, (g - high.astype(F32)).astype(BF16)


def without_self(s):
    same = lax.broadcasted_iota(jnp.int32, s.shape, 0) == lax.broadcasted_iota(
        jnp.int32, s.shape, 1
    )
    return jnp.where(same, FAR, s)


def pair_sums(pt, vt, qf, tf):
    zero = jnp.zeros((KF, 2 * SLOTS), BF16)
    block = jnp.zeros((SLOTS, SLOTS), BF16)

    def target(c, carry):
        x, y = c // (NY // 2), (c % (NY // 2)) * 2

        def query(col, t):
            at = pl.multiple_of(c * (4 * KF) + (2 * col + t) * KF, 8)
            return qf[pl.ds(at, KF), :].astype(BF16)

        def weights(s, left, right):
            rows = [zero] * PZ
            rows[s] = jnp.concatenate([left, right], 1)
            return jnp.concatenate(rows, 0)

        q = [[query(col, t) for t in range(2)] for col in range(2)]
        w_mid = [[weights(s, *q[col]) for s in (1, 2)] for col in range(2)]
        w_end = [weights(3 * t, q[0][t], q[1][t]) for t in range(2)]

        def lanes(k, n):
            return pl.ds(pl.multiple_of((y + k) * SLOTS, SLOTS), n * SLOTS)

        def rows(dx, k, n):
            return pl.ds(pl.multiple_of(((x + dx) * PY + y + k) * SLOTS, SLOTS), n * SLOTS)

        totals = {}

        def add(key, value):
            totals[key] = totals[key] + value if key in totals else value

        def mid_distances(dx, col):
            source = pt[rows(dx, col, 3), :]
            return [jnp.dot(source, w, preferred_element_type=F32) for w in w_mid[col]]

        def mid_sums(dx, col, pair):
            if dx == 1:
                cut = []
                for t, s in enumerate(pair):
                    at = s[SLOTS : 2 * SLOTS]
                    left, right = at[:, :SLOTS], at[:, SLOTS:]
                    if t == 0:
                        left = without_self(left)
                    else:
                        right = without_self(right)
                    at = jnp.concatenate([left, right], 1)
                    cut.append(jnp.concatenate([s[:SLOTS], at, s[2 * SLOTS :]], 0))
                pair = cut
            g = [parts2(s) for s in pair]
            high = jnp.concatenate([g[0][0], g[1][0]], 0)
            low = jnp.concatenate([g[0][1], g[1][1]], 0)
            v = jnp.concatenate([vt[x + dx, s, :, lanes(col, 3)] for s in (1, 2)], 1)
            add(("mid", col), jnp.dot(v, high, preferred_element_type=F32))
            add(("mid_low", col), jnp.dot(v[: 2 * VF], low, preferred_element_type=F32))

        def end_distances(dx, t):
            return jnp.dot(pt[rows(dx, 0, 4), :], w_end[t], preferred_element_type=F32)

        def end_sums(dx, t, s):
            left = parts2(s[: 3 * SLOTS, :SLOTS])
            right = parts2(s[SLOTS:, SLOTS:])
            high, low = [
                jnp.concatenate(
                    [jnp.concatenate([a, block], 0), jnp.concatenate([block, b], 0)], 1
                )
                for a, b in zip(left, right)
            ]
            v = vt[x + dx, 3 * t, :, lanes(0, 4)]
            add(("end", t), jnp.dot(v, high, preferred_element_type=F32))
            add(("end_low", t), jnp.dot(v[: 2 * VF], low, preferred_element_type=F32))

        waiting = None
        for dx in range(3):
            for k in range(2):
                for first, then in ((mid_distances, mid_sums), (end_distances, end_sums)):
                    made = (then, dx, k, first(dx, k))
                    if waiting is not None:
                        waiting[0](*waiting[1:])
                    waiting = made
        waiting[0](*waiting[1:])

        def whole(kind, k):
            high, low = totals[(kind, k)], totals[(kind + "_low", k)]
            total = high[2 * VF : 3 * VF]
            for part in (low, high):
                total = total + part[VF : 2 * VF]
            return total + low[:VF] + high[:VF]

        mids = [whole("mid", k) for k in range(2)]
        ends = [whole("end", k) for k in range(2)]
        for col in range(2):
            for t in range(2):
                sums = mids[col][:, t * SLOTS : (t + 1) * SLOTS]
                sums = sums + ends[t][:, col * SLOTS : (col + 1) * SLOTS]
                at = pl.multiple_of(c * (4 * VF) + (2 * col + t) * VF, 8)
                tf[pl.ds(at, VF), :] = sums
        return carry

    lax.fori_loop(0, NX * NY // 2, target, 0)


def forces_of(g, coords, loc_ref, tf):
    rows = pl.ds(g * 8, 8)
    line = [loc_ref[3 + a, rows, :] for a in range(3)]
    burg = [loc_ref[6 + a, rows, :] for a in range(3)]
    sums = [jnp.zeros((8, SLOTS), F32) for _ in range(4)]
    for m in range(3):
        for n in range(3):
            a = burg[m] * line[n]
            for k in range(4):
                at = g * (8 * VF) + 9 * k + 3 * m + n
                sums[k] = sums[k] + a * tf[pl.ds(at, 8, stride=VF), :]
    return [MU_SCALE * (coords[k] * sums[0] - sums[k + 1]) for k in range(3)]


def start_kernel(pad_ref, loc_ref, mob_ref, speed_ref, peak_ref, pf, vf, pt, vt, qf, tf):
    prepare_sources(pad_ref, None, pf, vf)
    lay_out_sources(pf, vf, pt, vt)
    every = prepare_targets(loc_ref, None, qf)
    pair_sums(pt, vt, qf, tf)
    peak = jnp.zeros((8, SLOTS), F32)
    for g in range(CELLS // 8):
        rows = pl.ds(g * 8, 8)
        force = forces_of(g, every[g], loc_ref, tf)
        mobility = mob_ref[rows, :]
        speed = [mobility * f for f in force]
        for a in range(3):
            speed_ref[a, rows, :] = speed[a]
        peak = jnp.maximum(
            peak, speed[0] * speed[0] + speed[1] * speed[1] + speed[2] * speed[2]
        )
    top = jnp.max(jnp.max(peak, axis=0, keepdims=True), axis=1, keepdims=True)
    peak_ref[...] = jnp.broadcast_to(top, peak_ref.shape)


def end_kernel(
    pad_ref, loc_ref, mob_ref, padv_ref, speed_ref, peak_ref, moved_ref, force_ref,
    pf, vf, pt, vt, qf, tf,
):
    peak = jnp.max(jnp.max(peak_ref[...], axis=0, keepdims=True), axis=1, keepdims=True)
    step = STEP_LIMIT * lax.rsqrt(jnp.broadcast_to(peak, (8, SLOTS)) + 1e-12)
    prepare_sources(pad_ref, (padv_ref, step), pf, vf)
    lay_out_sources(pf, vf, pt, vt)
    every = prepare_targets(loc_ref, (speed_ref, step), qf)
    pair_sums(pt, vt, qf, tf)
    for g in range(CELLS // 8):
        rows = pl.ds(g * 8, 8)
        force = forces_of(g, every[g], loc_ref, tf)
        mobility = mob_ref[rows, :]
        for a in range(3):
            force_ref[a, rows, :] = force[a]
            moved_ref[a, rows, :] = loc_ref[a, rows, :] + 0.5 * step * (
                speed_ref[a, rows, :] + mobility * force[a]
            )


def call(kernel, out_shapes, operands, name):
    whole = pl.BlockSpec(memory_space=pltpu.VMEM)
    return pl.pallas_call(
        kernel,
        out_shape=out_shapes,
        in_specs=[whole] * len(operands),
        out_specs=[whole] * len(out_shapes),
        scratch_shapes=[
            pltpu.VMEM((PADDED * KF, SLOTS), F32),
            pltpu.VMEM((PADDED * VF, SLOTS), F32),
            pltpu.VMEM((PX * PY * SLOTS, 128), BF16),
            pltpu.VMEM((PX, PZ, VROWS, PY * SLOTS), BF16),
            pltpu.VMEM((CELLS * KF, SLOTS), F32),
            pltpu.VMEM((CELLS * VF, SLOTS), F32),
        ],
        compiler_params=pltpu.CompilerParams(vmem_limit_bytes=48 << 20),
        name=name,
    )(*operands)


def on_device(positions, line_vectors, burgers, mobility, occupancy):
    slots = lax.broadcasted_iota(jnp.int32, mobility.shape, 3)
    live = (slots < occupancy[..., None]).astype(F32)
    fields = jnp.concatenate([positions, line_vectors, burgers * live], 0)
    sides = ((GX, 1), (GY, 2), ("gz", 3))
    pad = extended(fields, sides).reshape(9, PADDED, SLOTS)
    loc = fields.reshape(9, CELLS, SLOTS)
    mob = mobility.reshape(CELLS, SLOTS)
    devices = lax.axis_size(EVERY)
    vec = jax.ShapeDtypeStruct((3, CELLS, SLOTS), F32)
    speed, peaks = call(
        start_kernel,
        [vec, jax.ShapeDtypeStruct((devices, SLOTS), F32)],
        [pad, loc, mob],
        "start_forces",
    )
    peaks = lax.all_to_all(peaks.reshape(devices, 1, SLOTS), EVERY, 0, 0)
    peaks = peaks.reshape(devices, SLOTS)
    padv = extended(speed.reshape(3, NX, NY, NZ, SLOTS), sides).reshape(3, PADDED, SLOTS)
    moved, force = call(
        end_kernel, [vec, vec], [pad, loc, mob, padv, speed, peaks], "end_forces"
    )
    shape = (3, NX, NY, NZ, SLOTS)
    return moved.reshape(shape), force.reshape(shape)


def solution(mesh):
    finer = Mesh(
        mesh.devices.reshape(4, 2, 4, 2, mesh.shape["gz"]), ("gx_0", "gx_1", "gy_0", "gy_1", "gz")
    )
    in_specs = (
        P(None, GX, GY, "gz", None),
        P(None, GX, GY, "gz", None),
        P(None, GX, GY, "gz", None),
        P(GX, GY, "gz", None),
        P(GX, GY, "gz"),
    )
    out_specs = (P(None, GX, GY, "gz", None), P(None, GX, GY, "gz", None))
    return jax.shard_map(
        on_device, mesh=finer, in_specs=in_specs, out_specs=out_specs, check_vma=False
    )
```

```python
import functools

import jax
import jax.numpy as jnp
from jax import lax
from jax.experimental import pallas as pl
from jax.experimental.pallas import tpu as pltpu
from jax.sharding import Mesh
from jax.sharding import PartitionSpec as P

GX = ("gx_0", "gx_1")
GY = ("gy_0", "gy_1")
EVERY = ("gx_0", "gx_1", "gy_0", "gy_1", "gz")

CORE_SQUARED = 0.25
MU_SCALE = 0.05
CROSS_WEIGHT = 0.5
STEP_LIMIT = 0.1

NX, NY, NZ, SLOTS = 4, 4, 2, 128
PX, PY, PZ = NX + 2, NY + 2, NZ + 2
CELLS = NX * NY * NZ
PADDED = PX * PY * PZ
KF = 32
VF = 40
FAR = 3e38
VROWS = 128
F32 = jnp.float32
BF16 = jnp.bfloat16


def ring(axis):
    count = lax.axis_size(axis)
    forward = [(i, (i + 1) % count) for i in range(count)]
    return forward, [(t, s) for s, t in forward]


def extended(block, sides):
    for axis, dim in sides:
        forward, backward = ring(axis)
        size = block.shape[dim]
        low = lax.ppermute(lax.slice_in_dim(block, size - 1, size, axis=dim), axis, forward)
        high = lax.ppermute(lax.slice_in_dim(block, 0, 1, axis=dim), axis, backward)
        block = jnp.concatenate([low, block, high], axis=dim)
    return block


def parts3(v):
    high = v.astype(BF16).astype(F32)
    rest = v - high
    mid = rest.astype(BF16).astype(F32)
    return high, mid, rest - mid


def distance_features(coords, source):
    one = jnp.ones_like(coords[0])
    square = coords[0] * coords[0] + coords[1] * coords[1] + coords[2] * coords[2]
    rows = []
    for x in coords:
        h, m, l = parts3(x)
        if source:
            h, m, l = -2.0 * h, -2.0 * m, -2.0 * l
            rows += [h, h, m, m, h, l]
        else:
            rows += [h, m, h, m, l, h]
    if source:
        rows += [*parts3(square), one, one, one]
    else:
        rows += [one, one, one, *parts3(square + CORE_SQUARED)]
    return rows + [jnp.zeros_like(one)] * (KF - len(rows))


def prepare_sources(pad_ref, shift, pf, vf, inner):
    sub = lax.broadcasted_iota(jnp.int32, (8, SLOTS), 0)
    y_in = (sub >> 2).astype(F32)
    z_in = (sub & 3).astype(F32)

    def group(g, carry):
        rows = pl.ds(pl.multiple_of(g * 8, 8), 8)
        if inner:
            x0 = (g // 2).astype(F32) - float(PX // 2)
            y_at = y_in + (((g % 2) * 2 + 1).astype(F32) - float(PY // 2))
        else:
            x0 = g.astype(F32) - float(PX // 2)
            y_at = y_in * float(PY - 1) - float(PY // 2)
        pos = [pad_ref[a, rows, :] for a in range(3)]
        if shift is not None:
            padv_ref, step = shift
            pos = [pos[a] + step * padv_ref[a, rows, :] for a in range(3)]
        coords = [pos[0] + x0, pos[1] + y_at, pos[2] + (z_in - float(PZ // 2))]
        for f, row in enumerate(distance_features(coords, True)):
            pf[pl.ds(g * (8 * KF) + f, 8, stride=KF), :] = row
        line = [pad_ref[3 + a, rows, :] for a in range(3)]
        burg = [pad_ref[6 + a, rows, :] for a in range(3)]
        outer = [[burg[m] * line[n] for n in range(3)] for m in range(3)]
        for m in range(3):
            for n in range(3):
                b = outer[m][n] - CROSS_WEIGHT * outer[n][m]
                f = 3 * m + n
                vf[pl.ds(g * (8 * VF) + f, 8, stride=VF), :] = b
                for a in range(3):
                    at = g * (8 * VF) + 9 * (a + 1) + f
                    vf[pl.ds(at, 8, stride=VF), :] = b * coords[a]
        return carry

    lax.fori_loop(0, pad_ref.shape[1] // 8, group, 0)


def lay_out_sources(pf, vf, pt, vt):
    across = vt.shape[3] // SLOTS

    def column(c, carry):
        at = pl.multiple_of(c * 128, 128)
        pt[pl.ds(at, 128), :] = pf[pl.ds(at, 128), :].T.astype(BF16)
        x, y = c // across, c % across
        lanes = pl.ds(pl.multiple_of(y * SLOTS, SLOTS), SLOTS)
        for z in range(PZ):
            v = vf[pl.ds(pl.multiple_of(c * (PZ * VF) + z * VF, 8), VF), :]
            rows = [*parts3(v), jnp.zeros((VROWS - 3 * VF, SLOTS), F32)]
            vt[x, z, :, lanes] = jnp.concatenate(rows, 0).astype(BF16)
        return carry

    lax.fori_loop(0, PX * across, column, 0, unroll=6)


def prepare_targets(loc_ref, shift, qf):
    sub = lax.broadcasted_iota(jnp.int32, (8, SLOTS), 0)
    y_in = (sub >> 1).astype(F32)
    z_in = (sub & 1).astype(F32)
    every = []
    for g in range(CELLS // 8):
        rows = pl.ds(g * 8, 8)
        pos = [loc_ref[a, rows, :] for a in range(3)]
        if shift is not None:
            speed_ref, step = shift
            pos = [pos[a] + step * speed_ref[a, rows, :] for a in range(3)]
        coords = [
            pos[0] + float(g + 1 - PX // 2),
            pos[1] + (y_in + float(1 - PY // 2)),
            pos[2] + (z_in + float(1 - PZ // 2)),
        ]
        for f, row in enumerate(distance_features(coords, False)):
            qf[pl.ds(g * (8 * KF) + f, 8, stride=KF), :] = row
        every.append(coords)
    return every


def parts2(s):
    inverse = lax.rsqrt(s)
    g = inverse * inverse * inverse
    high = g.astype(BF16)
    return high, (g - high.astype(F32)).astype(BF16)


def without_self(s):
    same = lax.broadcasted_iota(jnp.int32, s.shape, 0) == lax.broadcasted_iota(
        jnp.int32, s.shape, 1
    )
    return jnp.where(same, FAR, s)


def chunks_of(inner):
    chunks = []
    if inner:
        for y in range(NY):
            low, high = max(y - 1, 0), min(y + 1, NY - 1)
            for dx in range(3):
                runs = [(dx, low, high - low + 1, s, True, True) for s in (1, 2)]
                chunks.append(((y, 0), (y, 1), runs))
            if y % 2 == 0:
                continue
            for t in range(2):
                runs = []
                for dx in range(3):
                    if y == 1:
                        runs.append((dx, 0, 2, 3 * t, True, True))
                        runs.append((dx, 2, 1, 3 * t, False, True))
                    else:
                        runs.append((dx, 1, 1, 3 * t, True, False))
                        runs.append((dx, 2, 2, 3 * t, True, True))
                chunks.append(((y - 1, t), (y, t), runs))
    else:
        for h, y in ((0, 0), (1, NY - 1)):
            runs = [(dx, h, 1, s, True, True) for dx in range(3) for s in (1, 2)]
            chunks.append(((y, 0), (y, 1), runs))
        for t in range(2):
            runs = [(dx, 0, 1, 3 * t, True, False) for dx in range(3)]
            runs += [(dx, 1, 1, 3 * t, False, True) for dx in range(3)]
            chunks.append(((0, t), (NY - 1, t), runs))
    return chunks


def pair_sums(pt, vt, qf, tf, inner, before=None):
    across = vt.shape[3] // SLOTS
    zero = jnp.zeros((KF, 2 * SLOTS), BF16)
    block = jnp.zeros((SLOTS, SLOTS), BF16)
    chunks = chunks_of(inner)

    def plane(x, carry):
        def query(y, t):
            at = pl.multiple_of(x * (NY * NZ * KF) + (y * NZ + t) * KF, 8)
            return qf[pl.ds(at, KF), :].astype(BF16)

        def distances(targets, runs):
            q = [query(*target) for target in targets]
            made = []
            for dx, first, count, s, to_left, to_right in runs:
                at = ((x + dx) * across + first) * SLOTS
                source = pt[pl.ds(pl.multiple_of(at, SLOTS), count * SLOTS), :]
                rows = [zero] * PZ
                rows[s] = jnp.concatenate(q, 1)
                if not (to_left and to_right):
                    rows = [r[:, :SLOTS] for r in rows]
                    rows[s] = q[0] if to_left else q[1]
                w = jnp.concatenate(rows, 0)
                made.append(jnp.dot(source, w, preferred_element_type=F32))
            return made

        def weights(targets, runs, made):
            high, low, v = [], [], []
            for (dx, first, count, s, to_left, to_right), r in zip(runs, made):
                both = to_left and to_right
                if dx == 1 and inner and both and s in (1, 2):
                    y = targets[0][0] - first
                    at = r[y * SLOTS : (y + 1) * SLOTS]
                    halves = [at[:, :SLOTS], at[:, SLOTS:]]
                    halves[s - 1] = without_self(halves[s - 1])
                    parts = [r[: y * SLOTS], jnp.concatenate(halves, 1), r[(y + 1) * SLOTS :]]
                    r = jnp.concatenate([p for p in parts if p.shape[0]], 0)
                for into, part in zip((high, low), parts2(r)):
                    if not both:
                        part = jnp.concatenate([part, block] if to_left else [block, part], 1)
                    into.append(part)
                v.append(vt[x + dx, s, :, first * SLOTS : (first + count) * SLOTS])
            return jnp.concatenate(v, 1), jnp.concatenate(high, 0), jnp.concatenate(low, 0)

        totals = {}

        def add(key, value):
            totals[key] = totals[key] + value if key in totals else value

        made = distances(chunks[0][:2], chunks[0][2])
        for n, (left, right, runs) in enumerate(chunks):
            coming = None
            if n + 1 < len(chunks):
                coming = distances(chunks[n + 1][:2], chunks[n + 1][2])
            v, high, low = weights((left, right), runs, made)
            add((left, right, 0), jnp.dot(v, high, preferred_element_type=F32))
            add((left, right, 1), jnp.dot(v[: 2 * VF], low, preferred_element_type=F32))
            made = coming

        cells = {}
        for left, right, kind in totals:
            if kind == 1:
                continue
            high, low = totals[(left, right, 0)], totals[(left, right, 1)]
            total = high[2 * VF : 3 * VF]
            for part in (low, high):
                total = total + part[VF : 2 * VF]
            total = total + low[:VF] + high[:VF]
            for k, cell in enumerate((left, right)):
                part = total[:, k * SLOTS : (k + 1) * SLOTS]
                cells[cell] = cells[cell] + part if cell in cells else part
        for y in range(NY):
            for t in range(NZ):
                at = pl.multiple_of(x * (NY * NZ * VF) + (y * NZ + t) * VF, 8)
                at = pl.ds(at, VF)
                if before is None:
                    tf[at, :] = cells[y, t]
                elif (y, t) in cells:
                    tf[at, :] = before[at, :] + cells[y, t]
                else:
                    tf[at, :] = before[at, :]
        return carry

    lax.fori_loop(0, NX, plane, 0)


def forces_of(g, coords, loc_ref, tf):
    rows = pl.ds(g * 8, 8)
    line = [loc_ref[3 + a, rows, :] for a in range(3)]
    burg = [loc_ref[6 + a, rows, :] for a in range(3)]
    sums = [jnp.zeros((8, SLOTS), F32) for _ in range(4)]
    for m in range(3):
        for n in range(3):
            a = burg[m] * line[n]
            for k in range(4):
                at = g * (8 * VF) + 9 * k + 3 * m + n
                sums[k] = sums[k] + a * tf[pl.ds(at, 8, stride=VF), :]
    return [MU_SCALE * (coords[k] * sums[0] - sums[k + 1]) for k in range(3)]


def step_of(peak_ref):
    peak = jnp.max(jnp.max(peak_ref[...], axis=0, keepdims=True), axis=1, keepdims=True)
    return STEP_LIMIT * lax.rsqrt(jnp.broadcast_to(peak, (8, SLOTS)) + 1e-12)


def start_inner(pad_ref, loc_ref, sums_ref, pf, vf, pt, vt, qf):
    prepare_sources(pad_ref, None, pf, vf, True)
    lay_out_sources(pf, vf, pt, vt)
    prepare_targets(loc_ref, None, qf)
    pair_sums(pt, vt, qf, sums_ref, True)


def end_inner(pad_ref, loc_ref, padv_ref, speed_ref, peak_ref, sums_ref, pf, vf, pt, vt, qf):
    step = step_of(peak_ref)
    prepare_sources(pad_ref, (padv_ref, step), pf, vf, True)
    lay_out_sources(pf, vf, pt, vt)
    prepare_targets(loc_ref, (speed_ref, step), qf)
    pair_sums(pt, vt, qf, sums_ref, True)


def start_outer(
    rim_ref, loc_ref, mob_ref, sums_ref, speed_ref, peak_ref, pf, vf, pt, vt, qf, tf
):
    prepare_sources(rim_ref, None, pf, vf, False)
    lay_out_sources(pf, vf, pt, vt)
    every = prepare_targets(loc_ref, None, qf)
    pair_sums(pt, vt, qf, tf, False, sums_ref)
    peak = jnp.zeros((8, SLOTS), F32)
    for g in range(CELLS // 8):
        rows = pl.ds(g * 8, 8)
        force = forces_of(g, every[g], loc_ref, tf)
        mobility = mob_ref[rows, :]
        speed = [mobility * f for f in force]
        for a in range(3):
            speed_ref[a, rows, :] = speed[a]
        peak = jnp.maximum(
            peak, speed[0] * speed[0] + speed[1] * speed[1] + speed[2] * speed[2]
        )
    top = jnp.max(jnp.max(peak, axis=0, keepdims=True), axis=1, keepdims=True)
    peak_ref[...] = jnp.broadcast_to(top, peak_ref.shape)


def end_outer(
    rim_ref, loc_ref, mob_ref, rimv_ref, speed_ref, peak_ref, sums_ref, moved_ref, force_ref,
    pf, vf, pt, vt, qf, tf,
):
    step = step_of(peak_ref)
    prepare_sources(rim_ref, (rimv_ref, step), pf, vf, False)
    lay_out_sources(pf, vf, pt, vt)
    every = prepare_targets(loc_ref, (speed_ref, step), qf)
    pair_sums(pt, vt, qf, tf, False, sums_ref)
    for g in range(CELLS // 8):
        rows = pl.ds(g * 8, 8)
        force = forces_of(g, every[g], loc_ref, tf)
        mobility = mob_ref[rows, :]
        for a in range(3):
            force_ref[a, rows, :] = force[a]
            moved_ref[a, rows, :] = loc_ref[a, rows, :] + 0.5 * step * (
                speed_ref[a, rows, :] + mobility * force[a]
            )


def call(kernel, out_shapes, operands, name, inner):
    whole = pl.BlockSpec(memory_space=pltpu.VMEM)
    across = NY if inner else PY - NY
    cells = PX * across * PZ
    scratch = [
        pltpu.VMEM((cells * KF, SLOTS), F32),
        pltpu.VMEM((cells * VF, SLOTS), F32),
        pltpu.VMEM((PX * across * SLOTS, 128), BF16),
        pltpu.VMEM((PX, PZ, VROWS, across * SLOTS), BF16),
        pltpu.VMEM((CELLS * KF, SLOTS), F32),
    ]
    if not inner:
        scratch.append(pltpu.VMEM((CELLS * VF, SLOTS), F32))
    return pl.pallas_call(
        kernel,
        out_shape=out_shapes,
        in_specs=[whole] * len(operands),
        out_specs=[whole] * len(out_shapes),
        scratch_shapes=scratch,
        compiler_params=pltpu.CompilerParams(vmem_limit_bytes=48 << 20),
        name=name,
    )(*operands)


VEC = jax.ShapeDtypeStruct((3, CELLS, SLOTS), F32)
SUMS = jax.ShapeDtypeStruct((CELLS * VF, SLOTS), F32)


def widened(block):
    block = extended(block, ((GX, 1), ("gz", 3)))
    forward, backward = ring(GY)
    low = lax.ppermute(block[:, :, NY - 1 :], GY, forward)
    high = lax.ppermute(block[:, :, :1], GY, backward)
    rim = jnp.concatenate([low, high], 2)
    count = block.shape[0]
    return block.reshape(count, PX * NY * PZ, SLOTS), rim.reshape(count, PX * 2 * PZ, SLOTS)


def on_device(positions, line_vectors, burgers, mobility, occupancy):
    slots = lax.broadcasted_iota(jnp.int32, mobility.shape, 3)
    live = (slots < occupancy[..., None]).astype(F32)
    fields = jnp.concatenate([positions, line_vectors, burgers * live], 0)
    pad, rim = widened(fields)
    loc = fields.reshape(9, CELLS, SLOTS)
    mob = mobility.reshape(CELLS, SLOTS)
    devices = lax.axis_size(EVERY)
    peaks = jax.ShapeDtypeStruct((devices, SLOTS), F32)
    (sums,) = call(start_inner, [SUMS], [pad, loc], "start_inner", True)
    speed, peaks = call(
        start_outer, [VEC, peaks], [rim, loc, mob, sums], "start_outer", False
    )
    peaks = lax.all_to_all(peaks.reshape(devices, 1, SLOTS), EVERY, 0, 0)
    peaks = peaks.reshape(devices, SLOTS)
    padv, rimv = widened(speed.reshape(3, NX, NY, NZ, SLOTS))
    (sums,) = call(end_inner, [SUMS], [pad, loc, padv, speed, peaks], "end_inner", True)
    moved, force = call(
        end_outer, [VEC, VEC], [rim, loc, mob, rimv, speed, peaks, sums], "end_outer", False
    )
    shape = (3, NX, NY, NZ, SLOTS)
    return moved.reshape(shape), force.reshape(shape)


def solution(mesh):
    finer = Mesh(
        mesh.devices.reshape(4, 2, 4, 2, mesh.shape["gz"]), ("gx_0", "gx_1", "gy_0", "gy_1", "gz")
    )
    in_specs = (
        P(None, GX, GY, "gz", None),
        P(None, GX, GY, "gz", None),
        P(None, GX, GY, "gz", None),
        P(GX, GY, "gz", None),
        P(GX, GY, "gz"),
    )
    out_specs = (P(None, GX, GY, "gz", None), P(None, GX, GY, "gz", None))
    return jax.shard_map(
        on_device, mesh=finer, in_specs=in_specs, out_specs=out_specs, check_vma=False
    )
```

```python
import functools

import jax
import jax.numpy as jnp
from jax import lax
from jax.experimental import pallas as pl
from jax.experimental.pallas import tpu as pltpu
from jax.sharding import Mesh
from jax.sharding import PartitionSpec as P

GX = ("gx_0", "gx_1")
GY = ("gy_0", "gy_1")
EVERY = ("gx_0", "gx_1", "gy_0", "gy_1", "gz")

CORE_SQUARED = 0.25
MU_SCALE = 0.05
CROSS_WEIGHT = 0.5
STEP_LIMIT = 0.1

NX, NY, NZ, SLOTS = 4, 4, 2, 128
PX, PY, PZ = NX + 2, NY + 2, NZ + 2
CELLS = NX * NY * NZ
PADDED = PX * PY * PZ
KF = 32
VF = 40
FAR = 3e38
VROWS = 128
F32 = jnp.float32
BF16 = jnp.bfloat16


def ring(axis):
    count = lax.axis_size(axis)
    forward = [(i, (i + 1) % count) for i in range(count)]
    return forward, [(t, s) for s, t in forward]


def extended(block, sides):
    for axis, dim in sides:
        forward, backward = ring(axis)
        size = block.shape[dim]
        low = lax.ppermute(lax.slice_in_dim(block, size - 1, size, axis=dim), axis, forward)
        high = lax.ppermute(lax.slice_in_dim(block, 0, 1, axis=dim), axis, backward)
        block = jnp.concatenate([low, block, high], axis=dim)
    return block


def parts3(v):
    high = v.astype(BF16).astype(F32)
    rest = v - high
    mid = rest.astype(BF16).astype(F32)
    return high, mid, rest - mid


def distance_features(coords, source):
    one = jnp.ones_like(coords[0])
    square = coords[0] * coords[0] + coords[1] * coords[1] + coords[2] * coords[2]
    rows = []
    for x in coords:
        h, m, l = parts3(x)
        if source:
            h, m, l = -2.0 * h, -2.0 * m, -2.0 * l
            rows += [h, h, m, m, h, l]
        else:
            rows += [h, m, h, m, l, h]
    if source:
        rows += [*parts3(square), one, one, one]
    else:
        rows += [one, one, one, *parts3(square + CORE_SQUARED)]
    return rows + [jnp.zeros_like(one)] * (KF - len(rows))


def prepare_sources(pad_ref, shift, pf, vf, rim=None):
    sub = lax.broadcasted_iota(jnp.int32, (8, SLOTS), 0)
    two = (sub >> 2).astype(F32)
    z_in = (sub & 3).astype(F32)
    first = 0 if rim is None else rim * PX * PZ

    def group(g, carry):
        rows = pl.ds(pl.multiple_of(g * 8, 8), 8)
        if rim is None:
            x_at = (g // 2).astype(F32) - float(PX // 2)
            y_at = two + (((g % 2) * 2 + 1).astype(F32) - float(PY // 2))
        else:
            x_at = two + ((g * 2).astype(F32) - float(PX // 2))
            y_at = float(rim * (PY - 1) - PY // 2)
        pos = [pad_ref[a, rows, :] for a in range(3)]
        if shift is not None:
            padv_ref, step = shift
            pos = [pos[a] + step * padv_ref[a, rows, :] for a in range(3)]
        coords = [pos[0] + x_at, pos[1] + y_at, pos[2] + (z_in - float(PZ // 2))]
        for f, row in enumerate(distance_features(coords, True)):
            pf[pl.ds(first * KF + g * (8 * KF) + f, 8, stride=KF), :] = row
        line = [pad_ref[3 + a, rows, :] for a in range(3)]
        burg = [pad_ref[6 + a, rows, :] for a in range(3)]
        outer = [[burg[m] * line[n] for n in range(3)] for m in range(3)]
        for m in range(3):
            for n in range(3):
                b = outer[m][n] - CROSS_WEIGHT * outer[n][m]
                f = 3 * m + n
                vf[pl.ds(first * VF + g * (8 * VF) + f, 8, stride=VF), :] = b
                for a in range(3):
                    at = first * VF + g * (8 * VF) + 9 * (a + 1) + f
                    vf[pl.ds(at, 8, stride=VF), :] = b * coords[a]
        return carry

    lax.fori_loop(0, pad_ref.shape[1] // 8, group, 0)


def lay_out_sources(pf, vf, pt, vt, inner):
    across = vt.shape[3] // SLOTS

    def column(c, carry):
        at = pl.multiple_of(c * 128, 128)
        pt[pl.ds(at, 128), :] = pf[pl.ds(at, 128), :].T.astype(BF16)
        x, y = (c // across, c % across) if inner else (c % PX, c // PX)
        lanes = pl.ds(pl.multiple_of(y * SLOTS, SLOTS), SLOTS)
        for z in range(PZ):
            v = vf[pl.ds(pl.multiple_of(c * (PZ * VF) + z * VF, 8), VF), :]
            rows = [*parts3(v), jnp.zeros((VROWS - 3 * VF, SLOTS), F32)]
            vt[x, z, :, lanes] = jnp.concatenate(rows, 0).astype(BF16)
        return carry

    lax.fori_loop(0, PX * across, column, 0, unroll=6)


def prepare_targets(loc_ref, shift, qf):
    sub = lax.broadcasted_iota(jnp.int32, (8, SLOTS), 0)
    y_in = (sub >> 1).astype(F32)
    z_in = (sub & 1).astype(F32)
    every = []
    for g in range(CELLS // 8):
        rows = pl.ds(g * 8, 8)
        pos = [loc_ref[a, rows, :] for a in range(3)]
        if shift is not None:
            speed_ref, step = shift
            pos = [pos[a] + step * speed_ref[a, rows, :] for a in range(3)]
        coords = [
            pos[0] + float(g + 1 - PX // 2),
            pos[1] + (y_in + float(1 - PY // 2)),
            pos[2] + (z_in + float(1 - PZ // 2)),
        ]
        for f, row in enumerate(distance_features(coords, False)):
            qf[pl.ds(g * (8 * KF) + f, 8, stride=KF), :] = row
        every.append(coords)
    return every


def parts2(s):
    inverse = lax.rsqrt(s)
    g = inverse * inverse * inverse
    high = g.astype(BF16)
    return high, (g - high.astype(F32)).astype(BF16)


def without_self(s):
    same = lax.broadcasted_iota(jnp.int32, s.shape, 0) == lax.broadcasted_iota(
        jnp.int32, s.shape, 1
    )
    return jnp.where(same, FAR, s)


def chunks_of(inner):
    chunks = []
    if inner:
        for y in range(NY):
            low, high = max(y - 1, 0), min(y + 1, NY - 1)
            for dx in range(3):
                runs = [(dx, low, high - low + 1, s, True, True) for s in (1, 2)]
                chunks.append(((y, 0), (y, 1), runs))
            if y % 2 == 0:
                continue
            for t in range(2):
                runs = []
                for dx in range(3):
                    if y == 1:
                        runs.append((dx, 0, 2, 3 * t, True, True))
                        runs.append((dx, 2, 1, 3 * t, False, True))
                    else:
                        runs.append((dx, 1, 1, 3 * t, True, False))
                        runs.append((dx, 2, 2, 3 * t, True, True))
                chunks.append(((y - 1, t), (y, t), runs))
    else:
        for h, y in ((0, 0), (1, NY - 1)):
            runs = [(dx, h, 1, s, True, True) for dx in range(3) for s in (1, 2)]
            chunks.append(((y, 0), (y, 1), runs))
        for t in range(2):
            runs = [(dx, 0, 1, 3 * t, True, False) for dx in range(3)]
            runs += [(dx, 1, 1, 3 * t, False, True) for dx in range(3)]
            chunks.append(((0, t), (NY - 1, t), runs))
    return chunks


def pair_sums(pt, vt, qf, tf, inner, before=None):
    across = vt.shape[3] // SLOTS
    zero = jnp.zeros((KF, 2 * SLOTS), BF16)
    block = jnp.zeros((SLOTS, SLOTS), BF16)
    chunks = chunks_of(inner)

    def plane(x, carry):
        def query(y, t):
            at = pl.multiple_of(x * (NY * NZ * KF) + (y * NZ + t) * KF, 8)
            return qf[pl.ds(at, KF), :].astype(BF16)

        def distances(targets, runs):
            q = [query(*target) for target in targets]
            made = []
            for dx, first, count, s, to_left, to_right in runs:
                at = (x + dx) * across + first if inner else first * PX + x + dx
                at = at * SLOTS
                source = pt[pl.ds(pl.multiple_of(at, SLOTS), count * SLOTS), :]
                rows = [zero] * PZ
                rows[s] = jnp.concatenate(q, 1)
                if not (to_left and to_right):
                    rows = [r[:, :SLOTS] for r in rows]
                    rows[s] = q[0] if to_left else q[1]
                w = jnp.concatenate(rows, 0)
                made.append(jnp.dot(source, w, preferred_element_type=F32))
            return made

        def weights(targets, runs, made):
            high, low, v = [], [], []
            for (dx, first, count, s, to_left, to_right), r in zip(runs, made):
                both = to_left and to_right
                if dx == 1 and inner and both and s in (1, 2):
                    y = targets[0][0] - first
                    at = r[y * SLOTS : (y + 1) * SLOTS]
                    halves = [at[:, :SLOTS], at[:, SLOTS:]]
                    halves[s - 1] = without_self(halves[s - 1])
                    parts = [r[: y * SLOTS], jnp.concatenate(halves, 1), r[(y + 1) * SLOTS :]]
                    r = jnp.concatenate([p for p in parts if p.shape[0]], 0)
                for into, part in zip((high, low), parts2(r)):
                    if not both:
                        part = jnp.concatenate([part, block] if to_left else [block, part], 1)
                    into.append(part)
                v.append(vt[x + dx, s, :, first * SLOTS : (first + count) * SLOTS])
            return jnp.concatenate(v, 1), jnp.concatenate(high, 0), jnp.concatenate(low, 0)

        totals = {}

        def add(key, value):
            totals[key] = totals[key] + value if key in totals else value

        made = distances(chunks[0][:2], chunks[0][2])
        for n, (left, right, runs) in enumerate(chunks):
            coming = None
            if n + 1 < len(chunks):
                coming = distances(chunks[n + 1][:2], chunks[n + 1][2])
            v, high, low = weights((left, right), runs, made)
            add((left, right, 0), jnp.dot(v, high, preferred_element_type=F32))
            add((left, right, 1), jnp.dot(v[: 2 * VF], low, preferred_element_type=F32))
            made = coming

        cells = {}
        for left, right, kind in totals:
            if kind == 1:
                continue
            high, low = totals[(left, right, 0)], totals[(left, right, 1)]
            total = high[2 * VF : 3 * VF]
            for part in (low, high):
                total = total + part[VF : 2 * VF]
            total = total + low[:VF] + high[:VF]
            for k, cell in enumerate((left, right)):
                part = total[:, k * SLOTS : (k + 1) * SLOTS]
                cells[cell] = cells[cell] + part if cell in cells else part
        for y in range(NY):
            for t in range(NZ):
                at = pl.multiple_of(x * (NY * NZ * VF) + (y * NZ + t) * VF, 8)
                at = pl.ds(at, VF)
                if before is None:
                    tf[at, :] = cells[y, t]
                elif (y, t) in cells:
                    tf[at, :] = before[at, :] + cells[y, t]
                else:
                    tf[at, :] = before[at, :]
        return carry

    lax.fori_loop(0, NX, plane, 0)


def forces_of(g, coords, loc_ref, tf):
    rows = pl.ds(g * 8, 8)
    line = [loc_ref[3 + a, rows, :] for a in range(3)]
    burg = [loc_ref[6 + a, rows, :] for a in range(3)]
    sums = [jnp.zeros((8, SLOTS), F32) for _ in range(4)]
    for m in range(3):
        for n in range(3):
            a = burg[m] * line[n]
            for k in range(4):
                at = g * (8 * VF) + 9 * k + 3 * m + n
                sums[k] = sums[k] + a * tf[pl.ds(at, 8, stride=VF), :]
    return [MU_SCALE * (coords[k] * sums[0] - sums[k + 1]) for k in range(3)]


def step_of(peak_ref):
    peak = jnp.max(jnp.max(peak_ref[...], axis=0, keepdims=True), axis=1, keepdims=True)
    return STEP_LIMIT * lax.rsqrt(jnp.broadcast_to(peak, (8, SLOTS)) + 1e-12)


def start_inner(pad_ref, loc_ref, sums_ref, pf, vf, pt, vt, qf):
    prepare_sources(pad_ref, None, pf, vf)
    lay_out_sources(pf, vf, pt, vt, True)
    prepare_targets(loc_ref, None, qf)
    pair_sums(pt, vt, qf, sums_ref, True)


def end_inner(pad_ref, loc_ref, padv_ref, speed_ref, peak_ref, sums_ref, pf, vf, pt, vt, qf):
    step = step_of(peak_ref)
    prepare_sources(pad_ref, (padv_ref, step), pf, vf)
    lay_out_sources(pf, vf, pt, vt, True)
    prepare_targets(loc_ref, (speed_ref, step), qf)
    pair_sums(pt, vt, qf, sums_ref, True)


def start_outer(
    low_ref, high_ref, loc_ref, mob_ref, sums_ref, speed_ref, peak_ref,
    pf, vf, pt, vt, qf, tf,
):
    prepare_sources(low_ref, None, pf, vf, 0)
    prepare_sources(high_ref, None, pf, vf, 1)
    lay_out_sources(pf, vf, pt, vt, False)
    every = prepare_targets(loc_ref, None, qf)
    pair_sums(pt, vt, qf, tf, False, sums_ref)
    peak = jnp.zeros((8, SLOTS), F32)
    for g in range(CELLS // 8):
        rows = pl.ds(g * 8, 8)
        force = forces_of(g, every[g], loc_ref, tf)
        mobility = mob_ref[rows, :]
        speed = [mobility * f for f in force]
        for a in range(3):
            speed_ref[a, rows, :] = speed[a]
        peak = jnp.maximum(
            peak, speed[0] * speed[0] + speed[1] * speed[1] + speed[2] * speed[2]
        )
    top = jnp.max(jnp.max(peak, axis=0, keepdims=True), axis=1, keepdims=True)
    peak_ref[...] = jnp.broadcast_to(top, peak_ref.shape)


def end_outer(
    low_ref, high_ref, loc_ref, mob_ref, lowv_ref, highv_ref, speed_ref, peak_ref, sums_ref,
    moved_ref, force_ref,
    pf, vf, pt, vt, qf, tf,
):
    step = step_of(peak_ref)
    prepare_sources(low_ref, (lowv_ref, step), pf, vf, 0)
    prepare_sources(high_ref, (highv_ref, step), pf, vf, 1)
    lay_out_sources(pf, vf, pt, vt, False)
    every = prepare_targets(loc_ref, (speed_ref, step), qf)
    pair_sums(pt, vt, qf, tf, False, sums_ref)
    for g in range(CELLS // 8):
        rows = pl.ds(g * 8, 8)
        force = forces_of(g, every[g], loc_ref, tf)
        mobility = mob_ref[rows, :]
        for a in range(3):
            force_ref[a, rows, :] = force[a]
            moved_ref[a, rows, :] = loc_ref[a, rows, :] + 0.5 * step * (
                speed_ref[a, rows, :] + mobility * force[a]
            )


def call(kernel, out_shapes, operands, name, inner):
    whole = pl.BlockSpec(memory_space=pltpu.VMEM)
    across = NY if inner else PY - NY
    cells = PX * across * PZ
    scratch = [
        pltpu.VMEM((cells * KF, SLOTS), F32),
        pltpu.VMEM((cells * VF, SLOTS), F32),
        pltpu.VMEM((PX * across * SLOTS, 128), BF16),
        pltpu.VMEM((PX, PZ, VROWS, across * SLOTS), BF16),
        pltpu.VMEM((CELLS * KF, SLOTS), F32),
    ]
    if not inner:
        scratch.append(pltpu.VMEM((CELLS * VF, SLOTS), F32))
    return pl.pallas_call(
        kernel,
        out_shape=out_shapes,
        in_specs=[whole] * len(operands),
        out_specs=[whole] * len(out_shapes),
        scratch_shapes=scratch,
        compiler_params=pltpu.CompilerParams(vmem_limit_bytes=48 << 20),
        name=name,
    )(*operands)


VEC = jax.ShapeDtypeStruct((3, CELLS, SLOTS), F32)
SUMS = jax.ShapeDtypeStruct((CELLS * VF, SLOTS), F32)


def widened(block):
    block = extended(block, ((GX, 1), ("gz", 3)))
    forward, backward = ring(GY)
    low = lax.ppermute(block[:, :, NY - 1 :], GY, forward)
    high = lax.ppermute(block[:, :, :1], GY, backward)
    rim = [plane.reshape(-1, PX * PZ, SLOTS) for plane in (low, high)]
    return block.reshape(-1, PX * NY * PZ, SLOTS), rim


def on_device(positions, line_vectors, burgers, mobility, occupancy):
    slots = lax.broadcasted_iota(jnp.int32, mobility.shape, 3)
    live = (slots < occupancy[..., None]).astype(F32)
    fields = jnp.concatenate([positions, line_vectors, burgers * live], 0)
    pad, rim = widened(fields)
    loc = fields.reshape(9, CELLS, SLOTS)
    mob = mobility.reshape(CELLS, SLOTS)
    devices = lax.axis_size(EVERY)
    peaks = jax.ShapeDtypeStruct((devices, SLOTS), F32)
    (sums,) = call(start_inner, [SUMS], [pad, loc], "start_inner", True)
    speed, peaks = call(
        start_outer, [VEC, peaks], [*rim, loc, mob, sums], "start_outer", False
    )
    peaks = lax.all_to_all(peaks.reshape(devices, 1, SLOTS), EVERY, 0, 0)
    peaks = peaks.reshape(devices, SLOTS)
    padv, rimv = widened(speed.reshape(3, NX, NY, NZ, SLOTS))
    (sums,) = call(end_inner, [SUMS], [pad, loc, padv, speed, peaks], "end_inner", True)
    moved, force = call(
        end_outer, [VEC, VEC], [*rim, loc, mob, *rimv, speed, peaks, sums], "end_outer", False
    )
    shape = (3, NX, NY, NZ, SLOTS)
    return moved.reshape(shape), force.reshape(shape)


def solution(mesh):
    finer = Mesh(
        mesh.devices.reshape(4, 2, 4, 2, mesh.shape["gz"]), ("gx_0", "gx_1", "gy_0", "gy_1", "gz")
    )
    in_specs = (
        P(None, GX, GY, "gz", None),
        P(None, GX, GY, "gz", None),
        P(None, GX, GY, "gz", None),
        P(GX, GY, "gz", None),
        P(GX, GY, "gz"),
    )
    out_specs = (P(None, GX, GY, "gz", None), P(None, GX, GY, "gz", None))
    return jax.shard_map(
        on_device, mesh=finer, in_specs=in_specs, out_specs=out_specs, check_vma=False
    )
```

```python
import functools

import jax
import jax.numpy as jnp
from jax import lax
from jax.experimental import pallas as pl
from jax.experimental.pallas import tpu as pltpu
from jax.sharding import Mesh
from jax.sharding import PartitionSpec as P

GX = ("gx_0", "gx_1")
GY = ("gy_0", "gy_1")
EVERY = ("gx_0", "gx_1", "gy_0", "gy_1", "gz")

CORE_SQUARED = 0.25
MU_SCALE = 0.05
CROSS_WEIGHT = 0.5
STEP_LIMIT = 0.1

NX, NY, NZ, SLOTS = 4, 4, 2, 128
PX, PY, PZ = NX + 2, NY + 2, NZ + 2
CELLS = NX * NY * NZ
PADDED = PX * PY * PZ
PER_INNER, PER_OUTER = 1, 4
KF = 32
VF = 40
FAR = 3e38
VROWS = 128
F32 = jnp.float32
BF16 = jnp.bfloat16


def ring(axis):
    count = lax.axis_size(axis)
    forward = [(i, (i + 1) % count) for i in range(count)]
    return forward, [(t, s) for s, t in forward]


def extended(block, sides):
    for axis, dim in sides:
        forward, backward = ring(axis)
        size = block.shape[dim]
        low = lax.ppermute(lax.slice_in_dim(block, size - 1, size, axis=dim), axis, forward)
        high = lax.ppermute(lax.slice_in_dim(block, 0, 1, axis=dim), axis, backward)
        block = jnp.concatenate([low, block, high], axis=dim)
    return block


def parts3(v):
    high = v.astype(BF16).astype(F32)
    rest = v - high
    mid = rest.astype(BF16).astype(F32)
    return high, mid, rest - mid


def distance_features(coords, source):
    one = jnp.ones_like(coords[0])
    square = coords[0] * coords[0] + coords[1] * coords[1] + coords[2] * coords[2]
    rows = []
    for x in coords:
        h, m, l = parts3(x)
        if source:
            h, m, l = -2.0 * h, -2.0 * m, -2.0 * l
            rows += [h, h, m, m, h, l]
        else:
            rows += [h, m, h, m, l, h]
    if source:
        rows += [*parts3(square), one, one, one]
    else:
        rows += [one, one, one, *parts3(square + CORE_SQUARED)]
    return rows + [jnp.zeros_like(one)] * (KF - len(rows))


def prepare_sources(pad_ref, shift, pf, vf, inner):
    sub = lax.broadcasted_iota(jnp.int32, (8, SLOTS), 0)
    y_in = (sub >> 2).astype(F32)
    z_in = (sub & 3).astype(F32)

    def group(g, carry):
        rows = pl.ds(pl.multiple_of(g * 8, 8), 8)
        if inner:
            x0 = (g // 2).astype(F32) - float(PX // 2)
            y_at = y_in + (((g % 2) * 2 + 1).astype(F32) - float(PY // 2))
        else:
            x0 = g.astype(F32) - float(PX // 2)
            y_at = y_in * float(PY - 1) - float(PY // 2)
        pos = [pad_ref[a, rows, :] for a in range(3)]
        if shift is not None:
            padv_ref, step = shift
            pos = [pos[a] + step * padv_ref[a, rows, :] for a in range(3)]
        coords = [pos[0] + x0, pos[1] + y_at, pos[2] + (z_in - float(PZ // 2))]
        for f, row in enumerate(distance_features(coords, True)):
            pf[pl.ds(g * (8 * KF) + f, 8, stride=KF), :] = row
        line = [pad_ref[3 + a, rows, :] for a in range(3)]
        burg = [pad_ref[6 + a, rows, :] for a in range(3)]
        outer = [[burg[m] * line[n] for n in range(3)] for m in range(3)]
        for m in range(3):
            for n in range(3):
                b = outer[m][n] - CROSS_WEIGHT * outer[n][m]
                f = 3 * m + n
                vf[pl.ds(g * (8 * VF) + f, 8, stride=VF), :] = b
                for a in range(3):
                    at = g * (8 * VF) + 9 * (a + 1) + f
                    vf[pl.ds(at, 8, stride=VF), :] = b * coords[a]
        return carry

    lax.fori_loop(0, pad_ref.shape[1] // 8, group, 0)


def lay_out_sources(pf, vf, pt, vt):
    across = vt.shape[3] // SLOTS

    def column(c, carry):
        at = pl.multiple_of(c * 128, 128)
        pt[pl.ds(at, 128), :] = pf[pl.ds(at, 128), :].T.astype(BF16)
        x, y = c // across, c % across
        lanes = pl.ds(pl.multiple_of(y * SLOTS, SLOTS), SLOTS)
        for z in range(PZ):
            v = vf[pl.ds(pl.multiple_of(c * (PZ * VF) + z * VF, 8), VF), :]
            rows = [*parts3(v), jnp.zeros((VROWS - 3 * VF, SLOTS), F32)]
            vt[x, z, :, lanes] = jnp.concatenate(rows, 0).astype(BF16)
        return carry

    lax.fori_loop(0, PX * across, column, 0, unroll=6)


def prepare_targets(loc_ref, shift, qf):
    sub = lax.broadcasted_iota(jnp.int32, (8, SLOTS), 0)
    y_in = (sub >> 1).astype(F32)
    z_in = (sub & 1).astype(F32)
    every = []
    for g in range(CELLS // 8):
        rows = pl.ds(g * 8, 8)
        pos = [loc_ref[a, rows, :] for a in range(3)]
        if shift is not None:
            speed_ref, step = shift
            pos = [pos[a] + step * speed_ref[a, rows, :] for a in range(3)]
        coords = [
            pos[0] + float(g + 1 - PX // 2),
            pos[1] + (y_in + float(1 - PY // 2)),
            pos[2] + (z_in + float(1 - PZ // 2)),
        ]
        for f, row in enumerate(distance_features(coords, False)):
            qf[pl.ds(g * (8 * KF) + f, 8, stride=KF), :] = row
        every.append(coords)
    return every


def parts2(s):
    inverse = lax.rsqrt(s)
    g = inverse * inverse * inverse
    high = g.astype(BF16)
    return high, (g - high.astype(F32)).astype(BF16)


def without_self(s):
    same = lax.broadcasted_iota(jnp.int32, s.shape, 0) == lax.broadcasted_iota(
        jnp.int32, s.shape, 1
    )
    return jnp.where(same, FAR, s)


def chunks_of(inner):
    chunks = []
    if inner:
        for y in range(NY):
            low, high = max(y - 1, 0), min(y + 1, NY - 1)
            for dx in range(3):
                runs = [(dx, low, high - low + 1, s, True, True) for s in (1, 2)]
                chunks.append(((y, 0), (y, 1), runs))
            if y % 2 == 0:
                continue
            for t in range(2):
                runs = []
                for dx in range(3):
                    if y == 1:
                        runs.append((dx, 0, 2, 3 * t, True, True))
                        runs.append((dx, 2, 1, 3 * t, False, True))
                    else:
                        runs.append((dx, 1, 1, 3 * t, True, False))
                        runs.append((dx, 2, 2, 3 * t, True, True))
                chunks.append(((y - 1, t), (y, t), runs))
    else:
        for h, y in ((0, 0), (1, NY - 1)):
            runs = [(dx, h, 1, s, True, True) for dx in range(3) for s in (1, 2)]
            chunks.append(((y, 0), (y, 1), runs))
        for t in range(2):
            runs = [(dx, 0, 1, 3 * t, True, False) for dx in range(3)]
            runs += [(dx, 1, 1, 3 * t, False, True) for dx in range(3)]
            chunks.append(((0, t), (NY - 1, t), runs))
    return chunks


def pair_sums(pt, vt, qf, tf, inner, before=None):
    across = vt.shape[3] // SLOTS
    zero = jnp.zeros((KF, 2 * SLOTS), BF16)
    block = jnp.zeros((SLOTS, SLOTS), BF16)
    chunks = chunks_of(inner)
    per = PER_INNER if inner else PER_OUTER

    def query(x, y, t):
        at = pl.multiple_of(x * (NY * NZ * KF) + (y * NZ + t) * KF, 8)
        return qf[pl.ds(at, KF), :].astype(BF16)

    def distances(x, left, right, runs):
        q = [query(x, *left), query(x, *right)]
        made = []
        for dx, first, count, s, to_left, to_right in runs:
            at = ((x + dx) * across + first) * SLOTS
            source = pt[pl.ds(pl.multiple_of(at, SLOTS), count * SLOTS), :]
            rows = [zero] * PZ
            rows[s] = jnp.concatenate(q, 1)
            if not (to_left and to_right):
                rows = [r[:, :SLOTS] for r in rows]
                rows[s] = q[0] if to_left else q[1]
            w = jnp.concatenate(rows, 0)
            made.append(jnp.dot(source, w, preferred_element_type=F32))
        return made

    def weights(x, left, runs, made):
        high, low, v = [], [], []
        for (dx, first, count, s, to_left, to_right), r in zip(runs, made):
            both = to_left and to_right
            if dx == 1 and inner and both and s in (1, 2):
                y = left[0] - first
                at = r[y * SLOTS : (y + 1) * SLOTS]
                halves = [at[:, :SLOTS], at[:, SLOTS:]]
                halves[s - 1] = without_self(halves[s - 1])
                parts = [r[: y * SLOTS], jnp.concatenate(halves, 1), r[(y + 1) * SLOTS :]]
                r = jnp.concatenate([p for p in parts if p.shape[0]], 0)
            for into, part in zip((high, low), parts2(r)):
                if not both:
                    part = jnp.concatenate([part, block] if to_left else [block, part], 1)
                into.append(part)
            v.append(vt[x + dx, s, :, first * SLOTS : (first + count) * SLOTS])
        return jnp.concatenate(v + v, 1), jnp.concatenate(high + low, 0)

    def step(n, carry):
        work = [(n * per + k, *chunk) for k in range(per) for chunk in chunks]
        totals = {}

        def add(key, value):
            totals[key] = totals[key] + value if key in totals else value

        made = distances(*work[0])
        for i, (x, left, right, runs) in enumerate(work):
            coming = distances(*work[i + 1]) if i + 1 < len(work) else None
            v, weighted = weights(x, left, runs, made)
            key = (i // len(chunks), left, right)
            add(key, jnp.dot(v, weighted, preferred_element_type=F32))
            made = coming

        cells = {}
        for (k, left, right), parts in totals.items():
            total = parts[2 * VF : 3 * VF] + parts[VF : 2 * VF] + parts[:VF]
            for half, cell in enumerate((left, right)):
                part = total[:, half * SLOTS : (half + 1) * SLOTS]
                cell = (k, *cell)
                cells[cell] = cells[cell] + part if cell in cells else part
        for k in range(per):
            for y in range(NY):
                for t in range(NZ):
                    at = (n * per + k) * (NY * NZ * VF) + (y * NZ + t) * VF
                    at = pl.ds(pl.multiple_of(at, 8), VF)
                    if before is None:
                        tf[at, :] = cells[k, y, t]
                    elif (k, y, t) in cells:
                        tf[at, :] = before[at, :] + cells[k, y, t]
                    else:
                        tf[at, :] = before[at, :]
        return carry

    lax.fori_loop(0, NX // per, step, 0)


def forces_of(g, coords, loc_ref, tf):
    rows = pl.ds(g * 8, 8)
    line = [loc_ref[3 + a, rows, :] for a in range(3)]
    burg = [loc_ref[6 + a, rows, :] for a in range(3)]
    sums = [jnp.zeros((8, SLOTS), F32) for _ in range(4)]
    for m in range(3):
        for n in range(3):
            a = burg[m] * line[n]
            for k in range(4):
                at = g * (8 * VF) + 9 * k + 3 * m + n
                sums[k] = sums[k] + a * tf[pl.ds(at, 8, stride=VF), :]
    return [MU_SCALE * (coords[k] * sums[0] - sums[k + 1]) for k in range(3)]


def step_of(peak_ref):
    peak = jnp.max(jnp.max(peak_ref[...], axis=0, keepdims=True), axis=1, keepdims=True)
    return STEP_LIMIT * lax.rsqrt(jnp.broadcast_to(peak, (8, SLOTS)) + 1e-12)


def start_inner(pad_ref, loc_ref, sums_ref, pf, vf, pt, vt, qf):
    prepare_sources(pad_ref, None, pf, vf, True)
    lay_out_sources(pf, vf, pt, vt)
    prepare_targets(loc_ref, None, qf)
    pair_sums(pt, vt, qf, sums_ref, True)


def end_inner(pad_ref, loc_ref, padv_ref, speed_ref, peak_ref, sums_ref, pf, vf, pt, vt, qf):
    step = step_of(peak_ref)
    prepare_sources(pad_ref, (padv_ref, step), pf, vf, True)
    lay_out_sources(pf, vf, pt, vt)
    prepare_targets(loc_ref, (speed_ref, step), qf)
    pair_sums(pt, vt, qf, sums_ref, True)


def start_outer(
    rim_ref, loc_ref, mob_ref, sums_ref, speed_ref, peak_ref, pf, vf, pt, vt, qf, tf
):
    prepare_sources(rim_ref, None, pf, vf, False)
    lay_out_sources(pf, vf, pt, vt)
    every = prepare_targets(loc_ref, None, qf)
    pair_sums(pt, vt, qf, tf, False, sums_ref)
    peak = jnp.zeros((8, SLOTS), F32)
    for g in range(CELLS // 8):
        rows = pl.ds(g * 8, 8)
        force = forces_of(g, every[g], loc_ref, tf)
        mobility = mob_ref[rows, :]
        speed = [mobility * f for f in force]
        for a in range(3):
            speed_ref[a, rows, :] = speed[a]
        peak = jnp.maximum(
            peak, speed[0] * speed[0] + speed[1] * speed[1] + speed[2] * speed[2]
        )
    top = jnp.max(jnp.max(peak, axis=0, keepdims=True), axis=1, keepdims=True)
    peak_ref[...] = jnp.broadcast_to(top, peak_ref.shape)


def end_outer(
    rim_ref, loc_ref, mob_ref, rimv_ref, speed_ref, peak_ref, sums_ref, moved_ref, force_ref,
    pf, vf, pt, vt, qf, tf,
):
    step = step_of(peak_ref)
    prepare_sources(rim_ref, (rimv_ref, step), pf, vf, False)
    lay_out_sources(pf, vf, pt, vt)
    every = prepare_targets(loc_ref, (speed_ref, step), qf)
    pair_sums(pt, vt, qf, tf, False, sums_ref)
    for g in range(CELLS // 8):
        rows = pl.ds(g * 8, 8)
        force = forces_of(g, every[g], loc_ref, tf)
        mobility = mob_ref[rows, :]
        for a in range(3):
            force_ref[a, rows, :] = force[a]
            moved_ref[a, rows, :] = loc_ref[a, rows, :] + 0.5 * step * (
                speed_ref[a, rows, :] + mobility * force[a]
            )


def call(kernel, out_shapes, operands, name, inner):
    whole = pl.BlockSpec(memory_space=pltpu.VMEM)
    across = NY if inner else PY - NY
    cells = PX * across * PZ
    scratch = [
        pltpu.VMEM((cells * KF, SLOTS), F32),
        pltpu.VMEM((cells * VF, SLOTS), F32),
        pltpu.VMEM((PX * across * SLOTS, 128), BF16),
        pltpu.VMEM((PX, PZ, VROWS, across * SLOTS), BF16),
        pltpu.VMEM((CELLS * KF, SLOTS), F32),
    ]
    if not inner:
        scratch.append(pltpu.VMEM((CELLS * VF, SLOTS), F32))
    return pl.pallas_call(
        kernel,
        out_shape=out_shapes,
        in_specs=[whole] * len(operands),
        out_specs=[whole] * len(out_shapes),
        scratch_shapes=scratch,
        compiler_params=pltpu.CompilerParams(vmem_limit_bytes=48 << 20),
        name=name,
    )(*operands)


VEC = jax.ShapeDtypeStruct((3, CELLS, SLOTS), F32)
SUMS = jax.ShapeDtypeStruct((CELLS * VF, SLOTS), F32)


def widened(block):
    block = extended(block, ((GX, 1), ("gz", 3)))
    forward, backward = ring(GY)
    low = lax.ppermute(block[:, :, NY - 1 :], GY, forward)
    high = lax.ppermute(block[:, :, :1], GY, backward)
    rim = jnp.concatenate([low, high], 2)
    count = block.shape[0]
    return block.reshape(count, PX * NY * PZ, SLOTS), rim.reshape(count, PX * 2 * PZ, SLOTS)


def on_device(positions, line_vectors, burgers, mobility, occupancy):
    slots = lax.broadcasted_iota(jnp.int32, mobility.shape, 3)
    live = (slots < occupancy[..., None]).astype(F32)
    fields = jnp.concatenate([positions, line_vectors, burgers * live], 0)
    pad, rim = widened(fields)
    loc = fields.reshape(9, CELLS, SLOTS)
    mob = mobility.reshape(CELLS, SLOTS)
    devices = lax.axis_size(EVERY)
    peaks = jax.ShapeDtypeStruct((devices, SLOTS), F32)
    (sums,) = call(start_inner, [SUMS], [pad, loc], "start_inner", True)
    speed, peaks = call(
        start_outer, [VEC, peaks], [rim, loc, mob, sums], "start_outer", False
    )
    peaks = lax.all_to_all(peaks.reshape(devices, 1, SLOTS), EVERY, 0, 0)
    peaks = peaks.reshape(devices, SLOTS)
    padv, rimv = widened(speed.reshape(3, NX, NY, NZ, SLOTS))
    (sums,) = call(end_inner, [SUMS], [pad, loc, padv, speed, peaks], "end_inner", True)
    moved, force = call(
        end_outer, [VEC, VEC], [rim, loc, mob, rimv, speed, peaks, sums], "end_outer", False
    )
    shape = (3, NX, NY, NZ, SLOTS)
    return moved.reshape(shape), force.reshape(shape)


def solution(mesh):
    finer = Mesh(
        mesh.devices.reshape(4, 2, 4, 2, mesh.shape["gz"]), ("gx_0", "gx_1", "gy_0", "gy_1", "gz")
    )
    in_specs = (
        P(None, GX, GY, "gz", None),
        P(None, GX, GY, "gz", None),
        P(None, GX, GY, "gz", None),
        P(GX, GY, "gz", None),
        P(GX, GY, "gz"),
    )
    out_specs = (P(None, GX, GY, "gz", None), P(None, GX, GY, "gz", None))
    return jax.shard_map(
        on_device, mesh=finer, in_specs=in_specs, out_specs=out_specs, check_vma=False
    )
```

```python
import functools

import jax
import jax.numpy as jnp
from jax import lax
from jax.experimental import pallas as pl
from jax.experimental.pallas import tpu as pltpu
from jax.sharding import Mesh
from jax.sharding import PartitionSpec as P

GX = ("gx_0", "gx_1")
GY = ("gy_0", "gy_1")
EVERY = ("gx_0", "gx_1", "gy_0", "gy_1", "gz")

CORE_SQUARED = 0.25
MU_SCALE = 0.05
CROSS_WEIGHT = 0.5
STEP_LIMIT = 0.1

NX, NY, NZ, SLOTS = 4, 4, 2, 128
PX, PY, PZ = NX + 2, NY + 2, NZ + 2
CELLS = NX * NY * NZ
PADDED = PX * PY * PZ
PER_INNER, PER_OUTER = 1, 4
KF = 32
VF = 40
FAR = 3e38
VROWS = 128
F32 = jnp.float32
BF16 = jnp.bfloat16


def ring(axis):
    count = lax.axis_size(axis)
    forward = [(i, (i + 1) % count) for i in range(count)]
    return forward, [(t, s) for s, t in forward]


def extended(block, sides):
    for axis, dim in sides:
        forward, backward = ring(axis)
        size = block.shape[dim]
        low = lax.ppermute(lax.slice_in_dim(block, size - 1, size, axis=dim), axis, forward)
        high = lax.ppermute(lax.slice_in_dim(block, 0, 1, axis=dim), axis, backward)
        block = jnp.concatenate([low, block, high], axis=dim)
    return block


def parts3(v):
    high = v.astype(BF16).astype(F32)
    rest = v - high
    mid = rest.astype(BF16).astype(F32)
    return high, mid, rest - mid


def distance_features(coords, source):
    one = jnp.ones_like(coords[0])
    square = coords[0] * coords[0] + coords[1] * coords[1] + coords[2] * coords[2]
    rows = []
    for x in coords:
        h, m, l = parts3(x)
        if source:
            h, m, l = -2.0 * h, -2.0 * m, -2.0 * l
            rows += [h, h, m, m, h, l]
        else:
            rows += [h, m, h, m, l, h]
    if source:
        rows += [*parts3(square), one, one, one]
    else:
        rows += [one, one, one, *parts3(square + CORE_SQUARED)]
    return rows + [jnp.zeros_like(one)] * (KF - len(rows))


def prepare_sources(pad_ref, shift, pf, vf, inner):
    sub = lax.broadcasted_iota(jnp.int32, (8, SLOTS), 0)
    y_in = (sub >> 2).astype(F32)
    z_in = (sub & 3).astype(F32)

    def group(g, carry):
        rows = pl.ds(pl.multiple_of(g * 8, 8), 8)
        if inner:
            x0 = (g // 2).astype(F32) - float(PX // 2)
            y_at = y_in + (((g % 2) * 2 + 1).astype(F32) - float(PY // 2))
        else:
            x0 = g.astype(F32) - float(PX // 2)
            y_at = y_in * float(PY - 1) - float(PY // 2)
        pos = [pad_ref[a, rows, :] for a in range(3)]
        if shift is not None:
            padv_ref, step = shift
            pos = [pos[a] + step * padv_ref[a, rows, :] for a in range(3)]
        coords = [pos[0] + x0, pos[1] + y_at, pos[2] + (z_in - float(PZ // 2))]
        for f, row in enumerate(distance_features(coords, True)):
            pf[pl.ds(g * (8 * KF) + f, 8, stride=KF), :] = row
        line = [pad_ref[3 + a, rows, :] for a in range(3)]
        burg = [pad_ref[6 + a, rows, :] for a in range(3)]
        outer = [[burg[m] * line[n] for n in range(3)] for m in range(3)]
        for m in range(3):
            for n in range(3):
                b = outer[m][n] - CROSS_WEIGHT * outer[n][m]
                f = 3 * m + n
                vf[pl.ds(g * (8 * VF) + f, 8, stride=VF), :] = b
                for a in range(3):
                    at = g * (8 * VF) + 9 * (a + 1) + f
                    vf[pl.ds(at, 8, stride=VF), :] = b * coords[a]
        return carry

    lax.fori_loop(0, pad_ref.shape[1] // 8, group, 0)


def lay_out_sources(pf, vf, pt, vt):
    across = vt.shape[3] // SLOTS

    def column(c, carry):
        at = pl.multiple_of(c * 128, 128)
        pt[pl.ds(at, 128), :] = pf[pl.ds(at, 128), :].T.astype(BF16)
        x, y = c // across, c % across
        lanes = pl.ds(pl.multiple_of(y * SLOTS, SLOTS), SLOTS)
        for z in range(PZ):
            v = vf[pl.ds(pl.multiple_of(c * (PZ * VF) + z * VF, 8), VF), :]
            rows = [*parts3(v), jnp.zeros((VROWS - 3 * VF, SLOTS), F32)]
            vt[x, z, :, lanes] = jnp.concatenate(rows, 0).astype(BF16)
        return carry

    lax.fori_loop(0, PX * across, column, 0, unroll=6)


def prepare_targets(loc_ref, shift, qf):
    sub = lax.broadcasted_iota(jnp.int32, (8, SLOTS), 0)
    y_in = (sub >> 1).astype(F32)
    z_in = (sub & 1).astype(F32)
    every = []
    for g in range(CELLS // 8):
        rows = pl.ds(g * 8, 8)
        pos = [loc_ref[a, rows, :] for a in range(3)]
        if shift is not None:
            speed_ref, step = shift
            pos = [pos[a] + step * speed_ref[a, rows, :] for a in range(3)]
        coords = [
            pos[0] + float(g + 1 - PX // 2),
            pos[1] + (y_in + float(1 - PY // 2)),
            pos[2] + (z_in + float(1 - PZ // 2)),
        ]
        for f, row in enumerate(distance_features(coords, False)):
            qf[pl.ds(g * (8 * KF) + f, 8, stride=KF), :] = row
        every.append(coords)
    return every


def parts2(s):
    inverse = lax.rsqrt(s)
    g = inverse * inverse * inverse
    high = g.astype(BF16)
    return high, (g - high.astype(F32)).astype(BF16)


def without_self(s):
    same = lax.broadcasted_iota(jnp.int32, s.shape, 0) == lax.broadcasted_iota(
        jnp.int32, s.shape, 1
    )
    return jnp.where(same, FAR, s)


def chunks_of(inner):
    chunks = []
    if inner:
        for y in range(NY):
            low, high = max(y - 1, 0), min(y + 1, NY - 1)
            for dx in range(3):
                runs = [(dx, low, high - low + 1, s, True, True) for s in (1, 2)]
                chunks.append(((y, 0), (y, 1), runs))
            if y % 2 == 0:
                continue
            for t in range(2):
                runs = []
                for dx in range(3):
                    if y == 1:
                        runs.append((dx, 0, 2, 3 * t, True, True))
                        runs.append((dx, 2, 1, 3 * t, False, True))
                    else:
                        runs.append((dx, 1, 1, 3 * t, True, False))
                        runs.append((dx, 2, 2, 3 * t, True, True))
                chunks.append(((y - 1, t), (y, t), runs))
    else:
        for h, y in ((0, 0), (1, NY - 1)):
            runs = [(dx, h, 1, s, True, True) for dx in range(3) for s in (1, 2)]
            chunks.append(((y, 0), (y, 1), runs))
        for t in range(2):
            runs = [(dx, 0, 1, 3 * t, True, False) for dx in range(3)]
            runs += [(dx, 1, 1, 3 * t, False, True) for dx in range(3)]
            chunks.append(((0, t), (NY - 1, t), runs))
    return chunks


def pair_sums(pt, vt, qf, tf, inner, before=None):
    across = vt.shape[3] // SLOTS
    zero = jnp.zeros((KF, 2 * SLOTS), BF16)
    block = jnp.zeros((SLOTS, SLOTS), BF16)
    chunks = chunks_of(inner)
    per = PER_INNER if inner else PER_OUTER

    def query(x, y, t):
        at = pl.multiple_of(x * (NY * NZ * KF) + (y * NZ + t) * KF, 8)
        return qf[pl.ds(at, KF), :].astype(BF16)

    def distances(x, left, right, runs):
        q = [query(x, *left), query(x, *right)]
        made = []
        for dx, first, count, s, to_left, to_right in runs:
            at = ((x + dx) * across + first) * SLOTS
            source = pt[pl.ds(pl.multiple_of(at, SLOTS), count * SLOTS), :]
            rows = [zero] * PZ
            rows[s] = jnp.concatenate(q, 1)
            if not (to_left and to_right):
                rows = [r[:, :SLOTS] for r in rows]
                rows[s] = q[0] if to_left else q[1]
            w = jnp.concatenate(rows, 0)
            made.append(jnp.dot(source, w, preferred_element_type=F32))
        return made

    def weights(x, left, runs, made):
        high, low, v = [], [], []
        for (dx, first, count, s, to_left, to_right), r in zip(runs, made):
            both = to_left and to_right
            if dx == 1 and inner and both and s in (1, 2):
                y = left[0] - first
                at = r[y * SLOTS : (y + 1) * SLOTS]
                halves = [at[:, :SLOTS], at[:, SLOTS:]]
                halves[s - 1] = without_self(halves[s - 1])
                parts = [r[: y * SLOTS], jnp.concatenate(halves, 1), r[(y + 1) * SLOTS :]]
                r = jnp.concatenate([p for p in parts if p.shape[0]], 0)
            for into, part in zip((high, low), parts2(r)):
                if not both:
                    part = jnp.concatenate([part, block] if to_left else [block, part], 1)
                into.append(part)
            v.append(vt[x + dx, s, :, first * SLOTS : (first + count) * SLOTS])
        return jnp.concatenate(v + v, 1), jnp.concatenate(high + low, 0)

    def step(n, carry):
        work = [(n * per + k, *chunk) for k in range(per) for chunk in chunks]
        totals = {}

        def add(key, value):
            totals[key] = totals[key] + value if key in totals else value

        made = distances(*work[0])
        for i, (x, left, right, runs) in enumerate(work):
            coming = distances(*work[i + 1]) if i + 1 < len(work) else None
            v, weighted = weights(x, left, runs, made)
            key = (i // len(chunks), left, right)
            add(key, jnp.dot(v, weighted, preferred_element_type=F32))
            made = coming

        cells = {}
        for (k, left, right), parts in totals.items():
            total = parts[2 * VF : 3 * VF] + parts[VF : 2 * VF] + parts[:VF]
            for half, cell in enumerate((left, right)):
                part = total[:, half * SLOTS : (half + 1) * SLOTS]
                cell = (k, *cell)
                cells[cell] = cells[cell] + part if cell in cells else part
        for k in range(per):
            for y in range(NY):
                for t in range(NZ):
                    at = (n * per + k) * (NY * NZ * VF) + (y * NZ + t) * VF
                    at = pl.ds(pl.multiple_of(at, 8), VF)
                    if before is None:
                        tf[at, :] = cells[k, y, t]
                    elif (k, y, t) in cells:
                        tf[at, :] = before[at, :] + cells[k, y, t]
                    else:
                        tf[at, :] = before[at, :]
        return carry

    lax.fori_loop(0, NX // per, step, 0)


def forces_of(g, coords, loc_ref, tf):
    rows = pl.ds(g * 8, 8)
    line = [loc_ref[3 + a, rows, :] for a in range(3)]
    burg = [loc_ref[6 + a, rows, :] for a in range(3)]
    sums = [jnp.zeros((8, SLOTS), F32) for _ in range(4)]
    for m in range(3):
        for n in range(3):
            a = burg[m] * line[n]
            for k in range(4):
                at = g * (8 * VF) + 9 * k + 3 * m + n
                sums[k] = sums[k] + a * tf[pl.ds(at, 8, stride=VF), :]
    return [MU_SCALE * (coords[k] * sums[0] - sums[k + 1]) for k in range(3)]


def step_of(peak_ref):
    peak = jnp.max(jnp.max(peak_ref[...], axis=0, keepdims=True), axis=1, keepdims=True)
    return STEP_LIMIT * lax.rsqrt(jnp.broadcast_to(peak, (8, SLOTS)) + 1e-12)


def start_inner(pad_ref, loc_ref, mob_ref, sums_ref, pf, vf, pt, vt, qf):
    prepare_sources(pad_ref, None, pf, vf, True)
    lay_out_sources(pf, vf, pt, vt)
    prepare_targets(loc_ref, None, qf)
    pair_sums(pt, vt, qf, sums_ref, True)


def end_inner(pad_ref, loc_ref, padv_ref, speed_ref, peak_ref, sums_ref, pf, vf, pt, vt, qf):
    step = step_of(peak_ref)
    prepare_sources(pad_ref, (padv_ref, step), pf, vf, True)
    lay_out_sources(pf, vf, pt, vt)
    prepare_targets(loc_ref, (speed_ref, step), qf)
    pair_sums(pt, vt, qf, sums_ref, True)


def start_outer(
    rim_ref, loc_ref, mob_ref, sums_ref, speed_ref, peak_ref, pf, vf, pt, vt, qf, tf
):
    prepare_sources(rim_ref, None, pf, vf, False)
    lay_out_sources(pf, vf, pt, vt)
    every = prepare_targets(loc_ref, None, qf)
    pair_sums(pt, vt, qf, tf, False, sums_ref)
    peak = jnp.zeros((8, SLOTS), F32)
    for g in range(CELLS // 8):
        rows = pl.ds(g * 8, 8)
        force = forces_of(g, every[g], loc_ref, tf)
        mobility = mob_ref[rows, :]
        speed = [mobility * f for f in force]
        for a in range(3):
            speed_ref[a, rows, :] = speed[a]
        peak = jnp.maximum(
            peak, speed[0] * speed[0] + speed[1] * speed[1] + speed[2] * speed[2]
        )
    top = jnp.max(jnp.max(peak, axis=0, keepdims=True), axis=1, keepdims=True)
    peak_ref[...] = jnp.broadcast_to(top, peak_ref.shape)


def end_outer(
    rim_ref, loc_ref, mob_ref, rimv_ref, speed_ref, peak_ref, sums_ref, moved_ref, force_ref,
    pf, vf, pt, vt, qf, tf,
):
    step = step_of(peak_ref)
    prepare_sources(rim_ref, (rimv_ref, step), pf, vf, False)
    lay_out_sources(pf, vf, pt, vt)
    every = prepare_targets(loc_ref, (speed_ref, step), qf)
    pair_sums(pt, vt, qf, tf, False, sums_ref)
    for g in range(CELLS // 8):
        rows = pl.ds(g * 8, 8)
        force = forces_of(g, every[g], loc_ref, tf)
        mobility = mob_ref[rows, :]
        for a in range(3):
            force_ref[a, rows, :] = force[a]
            moved_ref[a, rows, :] = loc_ref[a, rows, :] + 0.5 * step * (
                speed_ref[a, rows, :] + mobility * force[a]
            )


def call(kernel, out_shapes, operands, name, inner):
    whole = pl.BlockSpec(memory_space=pltpu.VMEM)
    across = NY if inner else PY - NY
    cells = PX * across * PZ
    scratch = [
        pltpu.VMEM((cells * KF, SLOTS), F32),
        pltpu.VMEM((cells * VF, SLOTS), F32),
        pltpu.VMEM((PX * across * SLOTS, 128), BF16),
        pltpu.VMEM((PX, PZ, VROWS, across * SLOTS), BF16),
        pltpu.VMEM((CELLS * KF, SLOTS), F32),
    ]
    if not inner:
        scratch.append(pltpu.VMEM((CELLS * VF, SLOTS), F32))
    return pl.pallas_call(
        kernel,
        out_shape=out_shapes,
        in_specs=[whole] * len(operands),
        out_specs=[whole] * len(out_shapes),
        scratch_shapes=scratch,
        compiler_params=pltpu.CompilerParams(vmem_limit_bytes=48 << 20),
        name=name,
    )(*operands)


VEC = jax.ShapeDtypeStruct((3, CELLS, SLOTS), F32)
SUMS = jax.ShapeDtypeStruct((CELLS * VF, SLOTS), F32)


def widened(block):
    block = extended(block, ((GX, 1), ("gz", 3)))
    forward, backward = ring(GY)
    low = lax.ppermute(block[:, :, NY - 1 :], GY, forward)
    high = lax.ppermute(block[:, :, :1], GY, backward)
    rim = jnp.concatenate([low, high], 2)
    count = block.shape[0]
    return block.reshape(count, PX * NY * PZ, SLOTS), rim.reshape(count, PX * 2 * PZ, SLOTS)


def on_device(positions, line_vectors, burgers, mobility, occupancy):
    fields = jnp.concatenate([positions, line_vectors, burgers], 0)
    row = lax.broadcasted_iota(jnp.int32, fields.shape, 0)
    slot = lax.broadcasted_iota(jnp.int32, fields.shape, 4)
    fields = jnp.where((row < 6) | (slot < occupancy[None, ..., None]), fields, 0.0)
    pad, rim = widened(fields)
    loc = fields.reshape(9, CELLS, SLOTS)
    mob = mobility.reshape(CELLS, SLOTS)
    devices = lax.axis_size(EVERY)
    peaks = jax.ShapeDtypeStruct((devices, SLOTS), F32)
    (sums,) = call(start_inner, [SUMS], [pad, loc, mob], "start_inner", True)
    speed, peaks = call(
        start_outer, [VEC, peaks], [rim, loc, mob, sums], "start_outer", False
    )
    peaks = lax.all_to_all(peaks.reshape(devices, 1, SLOTS), EVERY, 0, 0)
    peaks = peaks.reshape(devices, SLOTS)
    padv, rimv = widened(speed.reshape(3, NX, NY, NZ, SLOTS))
    (sums,) = call(end_inner, [SUMS], [pad, loc, padv, speed, peaks], "end_inner", True)
    moved, force = call(
        end_outer, [VEC, VEC], [rim, loc, mob, rimv, speed, peaks, sums], "end_outer", False
    )
    shape = (3, NX, NY, NZ, SLOTS)
    return moved.reshape(shape), force.reshape(shape)


def solution(mesh):
    finer = Mesh(
        mesh.devices.reshape(4, 2, 4, 2, mesh.shape["gz"]), ("gx_0", "gx_1", "gy_0", "gy_1", "gz")
    )
    in_specs = (
        P(None, GX, GY, "gz", None),
        P(None, GX, GY, "gz", None),
        P(None, GX, GY, "gz", None),
        P(GX, GY, "gz", None),
        P(GX, GY, "gz"),
    )
    out_specs = (P(None, GX, GY, "gz", None), P(None, GX, GY, "gz", None))
    return jax.shard_map(
        on_device, mesh=finer, in_specs=in_specs, out_specs=out_specs, check_vma=False
    )
```

```python
import functools

import jax
import jax.numpy as jnp
from jax import lax
from jax.experimental import pallas as pl
from jax.experimental.pallas import tpu as pltpu
from jax.sharding import Mesh
from jax.sharding import PartitionSpec as P

GX = ("gx_0", "gx_1")
GY = ("gy_0", "gy_1")
EVERY = ("gx_0", "gx_1", "gy_0", "gy_1", "gz")

CORE_SQUARED = 0.25
MU_SCALE = 0.05
CROSS_WEIGHT = 0.5
STEP_LIMIT = 0.1

NX, NY, NZ, SLOTS = 4, 4, 2, 128
PX, PY, PZ = NX + 2, NY + 2, NZ + 2
CELLS = NX * NY * NZ
PADDED = PX * PY * PZ
PER_INNER, PER_OUTER = 1, 4
KF = 32
VF = 40
FAR = 3e38
VROWS = 128
F32 = jnp.float32
BF16 = jnp.bfloat16


def ring(axis):
    count = lax.axis_size(axis)
    forward = [(i, (i + 1) % count) for i in range(count)]
    return forward, [(t, s) for s, t in forward]


def extended(block, sides):
    for axis, dim in sides:
        forward, backward = ring(axis)
        size = block.shape[dim]
        low = lax.ppermute(lax.slice_in_dim(block, size - 1, size, axis=dim), axis, forward)
        high = lax.ppermute(lax.slice_in_dim(block, 0, 1, axis=dim), axis, backward)
        block = jnp.concatenate([low, block, high], axis=dim)
    return block


def parts3(v):
    high = v.astype(BF16).astype(F32)
    rest = v - high
    mid = rest.astype(BF16).astype(F32)
    return high, mid, rest - mid


def distance_features(coords, source):
    one = jnp.ones_like(coords[0])
    square = coords[0] * coords[0] + coords[1] * coords[1] + coords[2] * coords[2]
    rows = []
    for x in coords:
        h, m, l = parts3(x)
        if source:
            h, m, l = -2.0 * h, -2.0 * m, -2.0 * l
            rows += [h, h, m, m, h, l]
        else:
            rows += [h, m, h, m, l, h]
    if source:
        rows += [*parts3(square), one, one, one]
    else:
        rows += [one, one, one, *parts3(square + CORE_SQUARED)]
    return rows + [jnp.zeros_like(one)] * (KF - len(rows))


def prepare_sources(pad_ref, shift, pf, vf, inner):
    sub = lax.broadcasted_iota(jnp.int32, (8, SLOTS), 0)
    y_in = (sub >> 2).astype(F32)
    z_in = (sub & 3).astype(F32)

    def group(g, carry):
        rows = pl.ds(pl.multiple_of(g * 8, 8), 8)
        if inner:
            x0 = (g // 2).astype(F32) - float(PX // 2)
            y_at = y_in + (((g % 2) * 2 + 1).astype(F32) - float(PY // 2))
        else:
            x0 = g.astype(F32) - float(PX // 2)
            y_at = y_in * float(PY - 1) - float(PY // 2)
        pos = [pad_ref[a, rows, :] for a in range(3)]
        if shift is not None:
            padv_ref, step = shift
            pos = [pos[a] + step * padv_ref[a, rows, :] for a in range(3)]
        coords = [pos[0] + x0, pos[1] + y_at, pos[2] + (z_in - float(PZ // 2))]
        for f, row in enumerate(distance_features(coords, True)):
            pf[pl.ds(g * (8 * KF) + f, 8, stride=KF), :] = row
        line = [pad_ref[3 + a, rows, :] for a in range(3)]
        burg = [pad_ref[6 + a, rows, :] for a in range(3)]
        outer = [[burg[m] * line[n] for n in range(3)] for m in range(3)]
        for m in range(3):
            for n in range(3):
                b = outer[m][n] - CROSS_WEIGHT * outer[n][m]
                f = 3 * m + n
                vf[pl.ds(g * (8 * VF) + f, 8, stride=VF), :] = b
                for a in range(3):
                    at = g * (8 * VF) + 9 * (a + 1) + f
                    vf[pl.ds(at, 8, stride=VF), :] = b * coords[a]
        return carry

    lax.fori_loop(0, pad_ref.shape[1] // 8, group, 0)


def lay_out_sources(pf, vf, pt, vt):
    across = vt.shape[3] // SLOTS

    def column(c, carry):
        at = pl.multiple_of(c * 128, 128)
        pt[pl.ds(at, 128), :] = pf[pl.ds(at, 128), :].T.astype(BF16)
        x, y = c // across, c % across
        lanes = pl.ds(pl.multiple_of(y * SLOTS, SLOTS), SLOTS)
        for z in range(PZ):
            v = vf[pl.ds(pl.multiple_of(c * (PZ * VF) + z * VF, 8), VF), :]
            rows = [*parts3(v), jnp.zeros((VROWS - 3 * VF, SLOTS), F32)]
            vt[x, z, :, lanes] = jnp.concatenate(rows, 0).astype(BF16)
        return carry

    lax.fori_loop(0, PX * across, column, 0, unroll=6)


def prepare_targets(loc_ref, shift, qf):
    sub = lax.broadcasted_iota(jnp.int32, (8, SLOTS), 0)
    y_in = (sub >> 1).astype(F32)
    z_in = (sub & 1).astype(F32)
    every = []
    for g in range(CELLS // 8):
        rows = pl.ds(g * 8, 8)
        pos = [loc_ref[a, rows, :] for a in range(3)]
        if shift is not None:
            speed_ref, step = shift
            pos = [pos[a] + step * speed_ref[a, rows, :] for a in range(3)]
        coords = [
            pos[0] + float(g + 1 - PX // 2),
            pos[1] + (y_in + float(1 - PY // 2)),
            pos[2] + (z_in + float(1 - PZ // 2)),
        ]
        for f, row in enumerate(distance_features(coords, False)):
            qf[pl.ds(g * (8 * KF) + f, 8, stride=KF), :] = row
        every.append(coords)
    return every


def parts2(s):
    inverse = lax.rsqrt(s)
    g = inverse * inverse * inverse
    high = g.astype(BF16)
    return high, (g - high.astype(F32)).astype(BF16)


def without_self(s):
    same = lax.broadcasted_iota(jnp.int32, s.shape, 0) == lax.broadcasted_iota(
        jnp.int32, s.shape, 1
    )
    return jnp.where(same, FAR, s)


def chunks_of(inner):
    chunks = []
    if inner:
        for y in range(NY):
            low, high = max(y - 1, 0), min(y + 1, NY - 1)
            for dx in range(3):
                runs = [(dx, low, high - low + 1, s, True, True) for s in (1, 2)]
                chunks.append(((y, 0), (y, 1), runs))
            if y % 2 == 0:
                continue
            for t in range(2):
                runs = []
                for dx in range(3):
                    if y == 1:
                        runs.append((dx, 0, 2, 3 * t, True, True))
                        runs.append((dx, 2, 1, 3 * t, False, True))
                    else:
                        runs.append((dx, 1, 1, 3 * t, True, False))
                        runs.append((dx, 2, 2, 3 * t, True, True))
                chunks.append(((y - 1, t), (y, t), runs))
    else:
        for h, y in ((0, 0), (1, NY - 1)):
            runs = [(dx, h, 1, s, True, True) for dx in range(3) for s in (1, 2)]
            chunks.append(((y, 0), (y, 1), runs))
        for t in range(2):
            runs = [(dx, 0, 1, 3 * t, True, False) for dx in range(3)]
            runs += [(dx, 1, 1, 3 * t, False, True) for dx in range(3)]
            chunks.append(((0, t), (NY - 1, t), runs))
    return chunks


def pair_sums(pt, vt, qf, tf, inner, before=None):
    across = vt.shape[3] // SLOTS
    zero = jnp.zeros((KF, 2 * SLOTS), BF16)
    block = jnp.zeros((SLOTS, SLOTS), BF16)
    chunks = chunks_of(inner)
    per = PER_INNER if inner else PER_OUTER

    def query(x, y, t):
        at = pl.multiple_of(x * (NY * NZ * KF) + (y * NZ + t) * KF, 8)
        return qf[pl.ds(at, KF), :].astype(BF16)

    def distances(x, left, right, runs):
        q = [query(x, *left), query(x, *right)]
        made = []
        for dx, first, count, s, to_left, to_right in runs:
            at = ((x + dx) * across + first) * SLOTS
            source = pt[pl.ds(pl.multiple_of(at, SLOTS), count * SLOTS), :]
            rows = [zero] * PZ
            rows[s] = jnp.concatenate(q, 1)
            if not (to_left and to_right):
                rows = [r[:, :SLOTS] for r in rows]
                rows[s] = q[0] if to_left else q[1]
            w = jnp.concatenate(rows, 0)
            made.append(jnp.dot(source, w, preferred_element_type=F32))
        return made

    def weights(x, left, runs, made):
        high, low, v = [], [], []
        for (dx, first, count, s, to_left, to_right), r in zip(runs, made):
            both = to_left and to_right
            if dx == 1 and inner and both and s in (1, 2):
                y = left[0] - first
                at = r[y * SLOTS : (y + 1) * SLOTS]
                halves = [at[:, :SLOTS], at[:, SLOTS:]]
                halves[s - 1] = without_self(halves[s - 1])
                parts = [r[: y * SLOTS], jnp.concatenate(halves, 1), r[(y + 1) * SLOTS :]]
                r = jnp.concatenate([p for p in parts if p.shape[0]], 0)
            for into, part in zip((high, low), parts2(r)):
                if not both:
                    part = jnp.concatenate([part, block] if to_left else [block, part], 1)
                into.append(part)
            v.append(vt[x + dx, s, :, first * SLOTS : (first + count) * SLOTS])
        return jnp.concatenate(v + v, 1), jnp.concatenate(high + low, 0)

    def step(n, carry):
        work = [(n * per + k, *chunk) for k in range(per) for chunk in chunks]
        totals = {}

        def add(key, value):
            totals[key] = totals[key] + value if key in totals else value

        made = distances(*work[0])
        for i, (x, left, right, runs) in enumerate(work):
            coming = distances(*work[i + 1]) if i + 1 < len(work) else None
            v, weighted = weights(x, left, runs, made)
            key = (i // len(chunks), left, right)
            add(key, jnp.dot(v, weighted, preferred_element_type=F32))
            made = coming

        cells = {}
        for (k, left, right), parts in totals.items():
            total = parts[2 * VF : 3 * VF] + parts[VF : 2 * VF] + parts[:VF]
            for half, cell in enumerate((left, right)):
                part = total[:, half * SLOTS : (half + 1) * SLOTS]
                cell = (k, *cell)
                cells[cell] = cells[cell] + part if cell in cells else part
        for k in range(per):
            for y in range(NY):
                for t in range(NZ):
                    at = (n * per + k) * (NY * NZ * VF) + (y * NZ + t) * VF
                    at = pl.ds(pl.multiple_of(at, 8), VF)
                    if before is None:
                        tf[at, :] = cells[k, y, t]
                    elif (k, y, t) in cells:
                        tf[at, :] = before[at, :] + cells[k, y, t]
                    else:
                        tf[at, :] = before[at, :]
        return carry

    lax.fori_loop(0, NX // per, step, 0)


def forces_of(g, coords, loc_ref, tf):
    rows = pl.ds(g * 8, 8)
    line = [loc_ref[3 + a, rows, :] for a in range(3)]
    burg = [loc_ref[6 + a, rows, :] for a in range(3)]
    sums = [jnp.zeros((8, SLOTS), F32) for _ in range(4)]
    for m in range(3):
        for n in range(3):
            a = burg[m] * line[n]
            for k in range(4):
                at = g * (8 * VF) + 9 * k + 3 * m + n
                sums[k] = sums[k] + a * tf[pl.ds(at, 8, stride=VF), :]
    return [MU_SCALE * (coords[k] * sums[0] - sums[k + 1]) for k in range(3)]


def step_of(peak_ref):
    peak = jnp.max(jnp.max(peak_ref[...], axis=0, keepdims=True), axis=1, keepdims=True)
    return STEP_LIMIT * lax.rsqrt(jnp.broadcast_to(peak, (8, SLOTS)) + 1e-12)


def start_inner(pad_ref, loc_ref, sums_ref, pf, vf, pt, vt, qf):
    prepare_sources(pad_ref, None, pf, vf, True)
    lay_out_sources(pf, vf, pt, vt)
    prepare_targets(loc_ref, None, qf)
    pair_sums(pt, vt, qf, sums_ref, True)


def end_inner(pad_ref, loc_ref, padv_ref, speed_ref, peak_ref, sums_ref, pf, vf, pt, vt, qf):
    step = step_of(peak_ref)
    prepare_sources(pad_ref, (padv_ref, step), pf, vf, True)
    lay_out_sources(pf, vf, pt, vt)
    prepare_targets(loc_ref, (speed_ref, step), qf)
    pair_sums(pt, vt, qf, sums_ref, True)


def start_outer(
    rim_ref, loc_ref, sums_ref, speed_ref, peak_ref, pf, vf, pt, vt, qf, tf
):
    prepare_sources(rim_ref, None, pf, vf, False)
    lay_out_sources(pf, vf, pt, vt)
    every = prepare_targets(loc_ref, None, qf)
    pair_sums(pt, vt, qf, tf, False, sums_ref)
    peak = jnp.zeros((8, SLOTS), F32)
    for g in range(CELLS // 8):
        rows = pl.ds(g * 8, 8)
        force = forces_of(g, every[g], loc_ref, tf)
        mobility = loc_ref[9, rows, :]
        speed = [mobility * f for f in force]
        for a in range(3):
            speed_ref[a, rows, :] = speed[a]
        peak = jnp.maximum(
            peak, speed[0] * speed[0] + speed[1] * speed[1] + speed[2] * speed[2]
        )
    top = jnp.max(jnp.max(peak, axis=0, keepdims=True), axis=1, keepdims=True)
    peak_ref[...] = jnp.broadcast_to(top, peak_ref.shape)


def end_outer(
    rim_ref, loc_ref, rimv_ref, speed_ref, peak_ref, sums_ref, moved_ref, force_ref,
    pf, vf, pt, vt, qf, tf,
):
    step = step_of(peak_ref)
    prepare_sources(rim_ref, (rimv_ref, step), pf, vf, False)
    lay_out_sources(pf, vf, pt, vt)
    every = prepare_targets(loc_ref, (speed_ref, step), qf)
    pair_sums(pt, vt, qf, tf, False, sums_ref)
    for g in range(CELLS // 8):
        rows = pl.ds(g * 8, 8)
        force = forces_of(g, every[g], loc_ref, tf)
        mobility = loc_ref[9, rows, :]
        for a in range(3):
            force_ref[a, rows, :] = force[a]
            moved_ref[a, rows, :] = loc_ref[a, rows, :] + 0.5 * step * (
                speed_ref[a, rows, :] + mobility * force[a]
            )


def call(kernel, out_shapes, operands, name, inner):
    whole = pl.BlockSpec(memory_space=pltpu.VMEM)
    across = NY if inner else PY - NY
    cells = PX * across * PZ
    scratch = [
        pltpu.VMEM((cells * KF, SLOTS), F32),
        pltpu.VMEM((cells * VF, SLOTS), F32),
        pltpu.VMEM((PX * across * SLOTS, 128), BF16),
        pltpu.VMEM((PX, PZ, VROWS, across * SLOTS), BF16),
        pltpu.VMEM((CELLS * KF, SLOTS), F32),
    ]
    if not inner:
        scratch.append(pltpu.VMEM((CELLS * VF, SLOTS), F32))
    return pl.pallas_call(
        kernel,
        out_shape=out_shapes,
        in_specs=[whole] * len(operands),
        out_specs=[whole] * len(out_shapes),
        scratch_shapes=scratch,
        compiler_params=pltpu.CompilerParams(vmem_limit_bytes=48 << 20),
        name=name,
    )(*operands)


VEC = jax.ShapeDtypeStruct((3, CELLS, SLOTS), F32)
SUMS = jax.ShapeDtypeStruct((CELLS * VF, SLOTS), F32)


def widened(block):
    block = extended(block, ((GX, 1), ("gz", 3)))
    forward, backward = ring(GY)
    low = lax.ppermute(block[:, :, NY - 1 :], GY, forward)
    high = lax.ppermute(block[:, :, :1], GY, backward)
    rim = jnp.concatenate([low, high], 2)
    count = block.shape[0]
    return block.reshape(count, PX * NY * PZ, SLOTS), rim.reshape(count, PX * 2 * PZ, SLOTS)


def on_device(positions, line_vectors, burgers, mobility, occupancy):
    fields = jnp.concatenate([positions, line_vectors, burgers], 0)
    row = lax.broadcasted_iota(jnp.int32, fields.shape, 0)
    slot = lax.broadcasted_iota(jnp.int32, fields.shape, 4)
    fields = jnp.where((row < 6) | (slot < occupancy[None, ..., None]), fields, 0.0)
    pad, rim = widened(fields)
    loc = jnp.concatenate([fields, mobility[None]], 0).reshape(10, CELLS, SLOTS)
    devices = lax.axis_size(EVERY)
    peaks = jax.ShapeDtypeStruct((devices, SLOTS), F32)
    (sums,) = call(start_inner, [SUMS], [pad, loc], "start_inner", True)
    speed, peaks = call(
        start_outer, [VEC, peaks], [rim, loc, sums], "start_outer", False
    )
    peaks = lax.all_to_all(peaks.reshape(devices, 1, SLOTS), EVERY, 0, 0)
    peaks = peaks.reshape(devices, SLOTS)
    padv, rimv = widened(speed.reshape(3, NX, NY, NZ, SLOTS))
    (sums,) = call(end_inner, [SUMS], [pad, loc, padv, speed, peaks], "end_inner", True)
    moved, force = call(
        end_outer, [VEC, VEC], [rim, loc, rimv, speed, peaks, sums], "end_outer", False
    )
    shape = (3, NX, NY, NZ, SLOTS)
    return moved.reshape(shape), force.reshape(shape)


def solution(mesh):
    finer = Mesh(
        mesh.devices.reshape(4, 2, 4, 2, mesh.shape["gz"]), ("gx_0", "gx_1", "gy_0", "gy_1", "gz")
    )
    in_specs = (
        P(None, GX, GY, "gz", None),
        P(None, GX, GY, "gz", None),
        P(None, GX, GY, "gz", None),
        P(GX, GY, "gz", None),
        P(GX, GY, "gz"),
    )
    out_specs = (P(None, GX, GY, "gz", None), P(None, GX, GY, "gz", None))
    return jax.shard_map(
        on_device, mesh=finer, in_specs=in_specs, out_specs=out_specs, check_vma=False
    )
```
